32 devices in a mesh: row: 4 (over y, x), col: 8 (over z, core).
Axes of the slice: x: 2, y: 2, z: 4, core: 2. Of those that a mesh axis runs over, the one named last changes fastest.
Arguments:
- xblocks: bfloat16 [56, 8, 128, 128], P('row', 'col'), may hold values from -2 to 2
- xcols: int32 [56, 8], P('row', 'col'), may hold values from 0 to 6, as said below
- outcols: int32 [56, 16], P('row', 'col'), may hold values from 0 to 6, as said below
Outputs:
- square_blocks: bfloat16 [56, 16, 128, 128], P('row', 'col')
The draws below stay inside these ranges and needn't reach their ends.
Inputs may be any that keep to these rules, and one draw needn't show every extreme that they name: xcols[m, t] is a block column within column tile t; over all block rows, the entries of one column tile take at most 3 distinct values. `outcols`: each entry names a block column of its column tile at which at least one block product of the window for that block row lands; entries of one row and tile may repeat.
All inputs are finite; a program needn't handle non-finite values.
Results may differ from the reference program's by a relative error of at most 0.001.
Values may be sent and summed in bfloat16 or wider, within the bound.
A program may use at most 64 MiB of HBM per device.

```python
import jax
import jax.numpy as jnp
from jax import lax

BS = 128
BLK_C = 7
KO = 2
LAND = 3
STEPS = 4
BLK_R = 14
NBLK = 56
N_ROW = 4
N_COL = 8


def draw_pattern(key):
    stride = BLK_C // LAND
    top_base = BLK_C - 1 - (LAND - 1) * stride
    base = jax.random.randint(jax.random.fold_in(key, 7), (N_COL,), 0, BLK_C, dtype=jnp.int32)
    base = base.at[0].set(top_base).at[1].set(0)
    steps_drawn = jax.random.randint(jax.random.fold_in(key, 11), (NBLK, N_COL), 0, LAND, dtype=jnp.int32)
    return ((base[None, :] + steps_drawn * stride) % BLK_C).astype(jnp.int32)


def draw_xcols(key, part):
    return draw_pattern(key)


def draw_outcols(key, part):
    pattern = draw_pattern(key)
    per_panel = N_COL // N_ROW
    count = STEPS * per_panel
    slots = jnp.arange(count, dtype=jnp.int32)
    step_ids = slots // per_panel
    half_ids = slots % per_panel
    grid_row = jnp.arange(NBLK, dtype=jnp.int32) // BLK_R
    panel = (grid_row[:, None] + step_ids[None, :]) % N_ROW
    tiles = per_panel * panel + half_ids[None, :]
    a_cols = jnp.take_along_axis(pattern, tiles, axis=1)
    b_rows = panel * BLK_R + half_ids[None, :] * BLK_C + a_cols
    landing = jnp.transpose(pattern[b_rows], (0, 2, 1))
    picks = jax.random.randint(jax.random.fold_in(key, 23), (NBLK, N_COL, KO), 0, count, dtype=jnp.int32)
    chosen = jnp.take_along_axis(landing, picks, axis=2)
    return chosen.reshape(NBLK, N_COL * KO).astype(jnp.int32)


def steps_of(own_key, shape, cuts, low, largest):
    def one(axis_at, shards_of):
        steps = jax.random.uniform(jax.random.fold_in(jax.random.fold_in(own_key, 6), axis_at), (shards_of,), jnp.float32, low / len(cuts), largest / len(cuts))
        return jnp.repeat(jnp.exp(steps), shape[axis_at] // shards_of).reshape((-1,) + (1,) * (len(shape) - axis_at - 1))

    level = one(*cuts[0])
    for cut in cuts[1:]:
        level = level * one(*cut)
    return level


def centred(stream_key, extent, scale, bound, pieces=(), kind=jnp.bfloat16):
    level = steps_of(stream_key, extent, pieces, -0.22, 0.18) if pieces else 1.0
    values = jax.random.normal(stream_key, extent, jnp.float32) * scale * level
    return jnp.minimum(jnp.maximum(values, -bound), bound).astype(kind)


def setup_inputs(seed: int = 0) -> dict:
    seeds = jax.random.split(jax.random.key(seed), 4)
    return {
        "xblocks": centred(seeds[0], (NBLK, N_COL, BS, BS), 0.3, 2.0, ((0, 4), (1, 8))),
        "xcols": draw_xcols(jax.random.fold_in(seeds[3], 71), 0),
        "outcols": draw_outcols(jax.random.fold_in(seeds[3], 71), 0),
    }


def reference(xblocks, xcols, outcols):
    per_panel = N_COL // N_ROW
    step_ids = jnp.arange(STEPS, dtype=jnp.int32)
    half_ids = jnp.arange(per_panel, dtype=jnp.int32)

    def one_row(block_row):
        grid_row = block_row // BLK_R
        panel = (grid_row + step_ids[:, None]) % N_ROW
        tiles = (per_panel * panel + half_ids[None, :]).reshape(-1).astype(jnp.int32)
        a_blocks = xblocks[block_row][tiles].astype(jnp.float32)
        a_cols = xcols[block_row][tiles]
        b_rows = ((panel * BLK_R + half_ids[None, :] * BLK_C).reshape(-1) + a_cols).astype(jnp.int32)
        b_blocks = xblocks[b_rows].astype(jnp.float32)
        landing = xcols[b_rows]
        targets = outcols[block_row].reshape(N_COL, KO)
        weight = (landing[:, :, None] == targets[None, :, :]).astype(jnp.float32)
        products = jnp.einsum('qab,qjbc->qjac', a_blocks, b_blocks, precision=lax.Precision.HIGHEST)
        summed = jnp.einsum('qjo,qjac->joac', weight, products, precision=lax.Precision.HIGHEST)
        return summed.reshape(N_COL * KO, BS, BS).astype(jnp.bfloat16)

    return lax.map(one_row, jnp.arange(NBLK, dtype=jnp.int32))
```

```python
import functools

import jax
import jax.numpy as jnp
from jax import lax
from jax.experimental import pallas as pl
from jax.experimental.pallas import tpu as pltpu
from jax.sharding import PartitionSpec as P

STEPS = 4
CORES = 2
PIECE = 4


def piece_sizes(rows):
    return tuple(min(PIECE, rows - start) for start in range(0, rows, PIECE))
MESH = pl.DeviceIdType.MESH


def passed_along(value, axis, steps):
    count = lax.axis_size(axis)
    pairs = [(source, (source + steps) % count) for source in range(count)]
    return lax.ppermute(value, axis, pairs)


def broadcast(value, axis, source):
    kept = jnp.where(lax.axis_index(axis) == source, value, 0).astype(value.dtype)
    return lax.psum(kept, axis)


def add_products(total, a_blocks, a_cols, b_blocks, b_cols, targets, offset):
    index = offset + a_cols
    picked = index[:, None] == jnp.arange(b_blocks.shape[0], dtype=jnp.int32)[None, :]
    chosen = jnp.einsum(
        "mr,rbc->mbc", picked.astype(b_blocks.dtype), b_blocks, preferred_element_type=jnp.float32
    ).astype(b_blocks.dtype)
    landing = jnp.sum(jnp.where(picked, b_cols[None, :], 0), axis=1)
    product = jnp.einsum("mab,mbc->mac", a_blocks, chosen, preferred_element_type=jnp.float32)
    weight = (landing[:, None] == targets).astype(jnp.float32)
    return total + weight[:, :, None, None] * product[:, None]


def on_any_mesh(xblocks, xcols, outcols):
    row_count = lax.axis_size("row")
    col_count = lax.axis_size("col")
    per_panel = col_count // row_count
    block_rows = xblocks.shape[0]
    tile_cols = block_rows // per_panel
    block_size = xblocks.shape[2]
    kept = outcols.shape[1]
    row_here = lax.axis_index("row")
    own_blocks = xblocks[:, 0]
    own_cols = xcols[:, 0]
    total = jnp.zeros((block_rows, kept, block_size, block_size), jnp.float32)
    moving = (own_blocks, own_cols)
    for step_no in range(STEPS):
        panel = (row_here + step_no) % row_count
        if step_no > 0:
            moving = passed_along((moving[0], moving[1]), "row", -1)
        for half_no in range(per_panel):
            tile_blocks, tile_cols_ids = (
                broadcast(own_blocks, "col", per_panel * panel + half_no),
                broadcast(own_cols, "col", per_panel * panel + half_no),
            )
            total = add_products(
                total,
                tile_blocks,
                tile_cols_ids,
                moving[0],
                moving[1],
                outcols,
                half_no * tile_cols,
            )
    return total.astype(jnp.bfloat16)


def remote(src, dst, send_sem, recv_sem, row, col):
    return pltpu.make_async_remote_copy(
        src_ref=src,
        dst_ref=dst,
        send_sem=send_sem,
        recv_sem=recv_sem,
        device_id=(row, col),
        device_id_type=MESH,
    )


def kernel(
    xc_ref, oc_ref, x_ref, o_ref,
    a_buf, b_buf, acc, meta_v, meta_s, oc_s,
    meta_loc, own_loc, ack,
    right_send, left_send, lane_recv, sib_send, sib_recv, meta_send,
    row_send, row_fwd, row_recv,
):
    rows = x_ref.shape[0]
    half = rows // 2
    chips = STEPS
    sizes = piece_sizes(rows)
    pieces = len(sizes)
    meta = pieces
    i = lax.axis_index("row")
    j = lax.axis_index("col")
    z, c = j // CORES, j % CORES
    y, x = i // 2, i % 2
    xn = 2 * y + (1 - x)
    yn = 2 * (1 - y) + x
    dg = 2 * (1 - y) + (1 - x)
    sib = j + 1 - 2 * c
    right, left = j + CORES, j - CORES
    inner_right = z < chips - 1
    inner_left = z > 0
    tiles = CORES * chips

    barrier = pltpu.get_barrier_semaphore()

    def greet(row, col):
        pl.semaphore_signal(barrier, inc=1, device_id=(row, col), device_id_type=MESH)

    def answer(k, row, col):
        pl.semaphore_signal(ack.at[k], inc=1, device_id=(row, col), device_id_type=MESH)

    greet(i, sib)
    pl.when(inner_right)(lambda: greet(i, right))
    pl.when(x == 0)(lambda: greet(xn, j))
    pl.when(y == 0)(lambda: greet(yn, j))

    own = pltpu.make_async_copy(x_ref.at[:, 0], a_buf.at[j], own_loc.at[0])
    own_b = pltpu.make_async_copy(x_ref.at[:, 0], b_buf.at[i], own_loc.at[1])
    own.start()
    own_b.start()
    oc_down = pltpu.make_async_copy(oc_ref, oc_s, own_loc.at[2])
    oc_down.start()
    own_meta = [
        pltpu.make_async_copy(xc_ref, meta_v.at[slot], own_loc.at[3 + n]) for n, slot in enumerate((j, tiles + i))
    ]
    for copy in own_meta:
        copy.start()
    pl.semaphore_wait(barrier, 1 + jnp.where(inner_left, 1, 0) + x + y)
    pl.when(inner_left)(lambda: answer(0, i, left))
    pl.when(x == 1)(lambda: answer(1, xn, j))
    pl.when(y == 1)(lambda: answer(2, yn, j))

    def part(k):
        return pl.ds(sum(sizes[:k]), sizes[k])

    def there(zs, core, k):
        if k == meta:
            return meta_v.at[CORES * zs + core]
        return a_buf.at[CORES * zs + core, part(k)]

    def here(d, zs, k):
        if d != 0:
            return there(zs, c, k)
        return xc_ref if k == meta else x_ref.at[part(k), 0]

    def to_right(d, zs, k):
        done = meta_send.at[0, d] if k == meta else right_send.at[d]
        return remote(here(d, zs, k), there(zs, c, k), done, lane_recv.at[zs, k], i, right)

    def to_left(d, zs, k):
        done = meta_send.at[1, d] if k == meta else left_send.at[d]
        return remote(here(d, zs, k), there(zs, c, k), done, lane_recv.at[zs, k], i, left)

    def sib_slot(d, k):
        return k if k == meta or d == chips - 1 else 0

    def to_sib(d, zs, k):
        done = meta_send.at[2, zs] if k == meta else sib_send.at[zs]
        return remote(here(d, zs, k), there(zs, c, k), done, sib_recv.at[zs, sib_slot(d, k)], i, sib)

    def lane_wait(zs, k):
        remote(there(zs, c, k), there(zs, c, k), sib_send.at[zs], lane_recv.at[zs, k], i, sib).wait_recv()

    def sib_wait(zs, k):
        mine = there(zs, 1 - c, k)
        remote(mine, mine, sib_send.at[zs], sib_recv.at[zs, k], i, sib).wait_recv()

    def sib_wait_whole(zs):
        mine = a_buf.at[CORES * zs + 1 - c]
        remote(mine, mine, sib_send.at[zs], sib_recv.at[zs, 0], i, sib).wait_recv()

    def sent_whole(sem):
        whole = a_buf.at[0]
        remote(whole, whole, sem, sib_recv.at[0, 0], i, sib).wait_send()

    def b_part(p, k):
        if k == 2:
            return meta_v.at[tiles + p]
        return b_buf.at[p, pl.ds(k * half, half)]

    def row_copy(n, k):
        source = xc_ref if k == 2 else x_ref.at[pl.ds(k * half, half), 0]
        return remote(source, b_part(i, k), row_send.at[n, k], row_recv.at[i, k], (xn, yn)[n], j)

    def row_wait(p, k):
        remote(b_part(p, k), b_part(p, k), row_fwd.at[0], row_recv.at[p, k], xn, j).wait_recv()

    def row_forward(n, k):
        p, to = ((xn, yn), (yn, xn))[n]
        return remote(b_part(p, k), b_part(p, k), row_fwd.at[k], row_recv.at[p, k], to, j)

    forwards = [row_forward(0, 0), row_forward(1, 1), row_forward(0, 2)]

    order = [0, meta, *range(1, pieces)]

    def out_left():
        for k in order:
            to_left(0, z, k).start()

    def out_right():
        pl.semaphore_wait(ack.at[0], 1)
        for k in order:
            to_right(0, z, k).start()

    def out_row(n):
        row_copy(n, 2).start()
        for k in range(2):
            row_copy(n, (k, 1 - k)[n]).start()

    pl.when(inner_left)(out_left)
    to_sib(0, z, meta).start()
    remote(x_ref.at[:, 0], a_buf.at[j], sib_send.at[z], sib_recv.at[z, 0], i, sib).start()
    pl.when(x == 1)(lambda: out_row(0))
    pl.when(y == 1)(lambda: out_row(1))
    pl.when(inner_right)(out_right)

    def late_row(n):
        pl.semaphore_wait(ack.at[1 + n], 1)
        out_row(n)

    pl.when(x == 0)(lambda: late_row(0))
    pl.when(y == 0)(lambda: late_row(1))

    def from_left(d, k):
        lane_wait(z - d, k)
        if d < chips - 1:
            pl.when(inner_right)(lambda: to_right(d, z - d, k).start())
        to_sib(d, z - d, k).start()

    def from_right(d, k):
        lane_wait(z + d, k)
        if d < chips - 1:
            pl.when(inner_left)(lambda: to_left(d, z + d, k).start())
        to_sib(d, z + d, k).start()

    def arrive(d, k):
        pl.when(z - d >= 0)(lambda: from_left(d, k))
        pl.when(z + d <= chips - 1)(lambda: from_right(d, k))

    def arrive_loop(d):
        arrive(d, 0)
        arrive(d, meta)
        for k in range(1, pieces):
            arrive(d, k)

    arrive_loop(1)
    row_wait(xn, 2)
    forwards[2].start()
    row_wait(xn, 0)
    forwards[0].start()
    row_wait(yn, 1)
    forwards[1].start()
    arrive_loop(2)
    row_wait(yn, 2)
    row_wait(dg, 2)
    row_wait(xn, 1)
    row_wait(yn, 0)
    row_wait(dg, 0)
    row_wait(dg, 1)
    own.wait()
    own_b.wait()
    oc_down.wait()
    for copy in own_meta:
        copy.wait()

    first = z // 2
    far = (chips - 1) * (1 - first)

    def near(n):
        return n + first

    def lower(start, count):
        down = pltpu.make_async_copy(meta_v.at[pl.ds(start, count)], meta_s.at[pl.ds(start, count)], meta_loc)
        down.start()
        down.wait()

    for n in range(chips - 1):
        sib_wait(near(n), meta)
    lower(CORES * first, CORES * (chips - 1))
    lower(tiles, chips)

    def operands(m, zs):
        lhs, rhs = [], []
        for h in range(CORES):
            t = CORES * zs + h
            at = h * half + meta_s[t, 0, m]
            block = b_buf[zs, at]
            landing = meta_s[tiles + zs, 0, at]
            zero = jnp.zeros_like(block)
            rhs.append(
                jnp.concatenate([jnp.where(landing == oc_s[o, m], block, zero) for o in range(2)], axis=1)
            )
            lhs.append(a_buf[t, m])
        return lhs, rhs

    def product(m, sources):
        lhs, rhs = [], []
        for zs in sources:
            more = operands(m, zs)
            lhs += more[0]
            rhs += more[1]
        return jnp.dot(
            jnp.concatenate(lhs, axis=1), jnp.concatenate(rhs, axis=0), preferred_element_type=jnp.float32
        )

    for n in range(chips - 1):
        sib_wait_whole(near(n))

    def early(m, carry):
        acc[m] = product(m, [near(n) for n in range(chips - 1)])
        return carry

    lax.fori_loop(0, rows, early, 0)

    is_end = jnp.logical_or(z == 0, z == chips - 1)
    not_end = jnp.logical_not(is_end)

    def far_arrive(k):
        pl.when(z == chips - 1)(lambda: from_left(chips - 1, k))
        pl.when(z == 0)(lambda: from_right(chips - 1, k))

    far_arrive(0)
    far_arrive(meta)

    for d in range(chips - 1):
        go_right = jnp.logical_and(inner_right, z - d >= 0)
        go_left = jnp.logical_and(inner_left, z + d <= chips - 1)
        pl.when(go_right)(lambda d=d: to_right(d, z - d, meta).wait_send())
        pl.when(go_left)(lambda d=d: to_left(d, z + d, meta).wait_send())
        if d < chips - 2:
            pl.when(go_right)(lambda d=d: sent_whole(right_send.at[d]))
            pl.when(go_left)(lambda d=d: sent_whole(left_send.at[d]))
        sent_whole(sib_send.at[near(d)])
        to_sib(1, near(d), meta).wait_send()
    to_sib(1, far, meta).wait_send()
    for k in range(3):
        for n in range(2):
            row_copy(n, k).wait_send()
        forwards[k].wait_send()

    sib_wait(far, meta)
    lower(CORES * far, CORES)
    pl.when(not_end)(lambda: sib_wait_whole(far))

    def late(m, carry):
        total = acc[m] + product(m, [far])
        for o in range(2):
            o_ref[m, o] = total[:, o * 128 : (o + 1) * 128].astype(o_ref.dtype)
        return carry

    for k in range(pieces):
        if k < pieces - 1:
            far_arrive(k + 1)
        pl.when(is_end)(lambda k=k: sib_wait(far, k))
        start = sum(sizes[:k])
        lax.fori_loop(start, start + sizes[k], late, 0, unroll=True)

    d = chips - 2
    pl.when(jnp.logical_and(inner_right, z - d >= 0))(lambda: sent_whole(right_send.at[d]))
    pl.when(jnp.logical_and(inner_left, z + d <= chips - 1))(lambda: sent_whole(left_send.at[d]))
    sent_whole(sib_send.at[far])


def on_four_by_eight(xblocks, xcols, outcols):
    rows, _, size, _ = xblocks.shape
    kept = outcols.shape[1]
    slots = CORES * STEPS + STEPS
    pieces = len(piece_sizes(rows))
    dma = pltpu.SemaphoreType.DMA
    return pl.pallas_call(
        kernel,
        out_shape=jax.ShapeDtypeStruct((rows, kept, size, size), jnp.bfloat16),
        in_specs=[
            pl.BlockSpec(memory_space=pltpu.HBM),
            pl.BlockSpec(memory_space=pltpu.HBM),
            pl.BlockSpec(memory_space=pltpu.HBM),
        ],
        out_specs=pl.BlockSpec(memory_space=pltpu.VMEM),
        scratch_shapes=[
            pltpu.VMEM((CORES * STEPS, rows, size, size), jnp.bfloat16),
            pltpu.VMEM((STEPS, rows, size, size), jnp.bfloat16),
            pltpu.VMEM((rows, size, kept * size), jnp.float32),
            pltpu.VMEM((slots, 1, rows), jnp.int32),
            pltpu.SMEM((slots, 1, rows), jnp.int32),
            pltpu.SMEM((kept, rows), jnp.int32),
            dma,
            dma((5,)),
            pltpu.SemaphoreType.REGULAR((3,)),
            dma((STEPS,)),
            dma((STEPS,)),
            dma((STEPS, pieces + 1)),
            dma((STEPS,)),
            dma((STEPS, pieces + 1)),
            dma((3, STEPS)),
            dma((2, 3)),
            dma((3,)),
            dma((STEPS, 3)),
        ],
        compiler_params=pltpu.CompilerParams(
            collective_id=0, has_side_effects=True, vmem_limit_bytes=32 * 1024 * 1024
        ),
    )(xcols.T, outcols.T, xblocks)


def solution(mesh):
    in_specs = (P("row", "col", None, None), P("row", "col"), P("row", "col"))
    out_specs = P("row", "col", None, None)
    fits = mesh.shape["row"] == STEPS and mesh.shape["col"] == CORES * STEPS
    body = on_four_by_eight if fits else on_any_mesh
    return jax.shard_map(body, mesh=mesh, in_specs=in_specs, out_specs=out_specs, check_vma=False)
```

```python
import functools

import jax
import jax.numpy as jnp
from jax import lax
from jax.experimental import pallas as pl
from jax.experimental.pallas import tpu as pltpu
from jax.sharding import PartitionSpec as P

STEPS = 4
CORES = 2
PIECE = 4


def piece_sizes(rows):
    return tuple(min(PIECE, rows - start) for start in range(0, rows, PIECE))
MESH = pl.DeviceIdType.MESH


def passed_along(value, axis, steps):
    count = lax.axis_size(axis)
    pairs = [(source, (source + steps) % count) for source in range(count)]
    return lax.ppermute(value, axis, pairs)


def broadcast(value, axis, source):
    kept = jnp.where(lax.axis_index(axis) == source, value, 0).astype(value.dtype)
    return lax.psum(kept, axis)


def add_products(total, a_blocks, a_cols, b_blocks, b_cols, targets, offset):
    index = offset + a_cols
    picked = index[:, None] == jnp.arange(b_blocks.shape[0], dtype=jnp.int32)[None, :]
    chosen = jnp.einsum(
        "mr,rbc->mbc", picked.astype(b_blocks.dtype), b_blocks, preferred_element_type=jnp.float32
    ).astype(b_blocks.dtype)
    landing = jnp.sum(jnp.where(picked, b_cols[None, :], 0), axis=1)
    product = jnp.einsum("mab,mbc->mac", a_blocks, chosen, preferred_element_type=jnp.float32)
    weight = (landing[:, None] == targets).astype(jnp.float32)
    return total + weight[:, :, None, None] * product[:, None]


def on_any_mesh(xblocks, xcols, outcols):
    row_count = lax.axis_size("row")
    col_count = lax.axis_size("col")
    per_panel = col_count // row_count
    block_rows = xblocks.shape[0]
    tile_cols = block_rows // per_panel
    block_size = xblocks.shape[2]
    kept = outcols.shape[1]
    row_here = lax.axis_index("row")
    own_blocks = xblocks[:, 0]
    own_cols = xcols[:, 0]
    total = jnp.zeros((block_rows, kept, block_size, block_size), jnp.float32)
    moving = (own_blocks, own_cols)
    for step_no in range(STEPS):
        panel = (row_here + step_no) % row_count
        if step_no > 0:
            moving = passed_along((moving[0], moving[1]), "row", -1)
        for half_no in range(per_panel):
            tile_blocks, tile_cols_ids = (
                broadcast(own_blocks, "col", per_panel * panel + half_no),
                broadcast(own_cols, "col", per_panel * panel + half_no),
            )
            total = add_products(
                total,
                tile_blocks,
                tile_cols_ids,
                moving[0],
                moving[1],
                outcols,
                half_no * tile_cols,
            )
    return total.astype(jnp.bfloat16)


def remote(src, dst, send_sem, recv_sem, row, col):
    return pltpu.make_async_remote_copy(
        src_ref=src,
        dst_ref=dst,
        send_sem=send_sem,
        recv_sem=recv_sem,
        device_id=(row, col),
        device_id_type=MESH,
    )


def kernel(
    xc_ref, oc_ref, x_ref, o_ref,
    a_buf, b_buf, acc, meta_v, meta_s, oc_s,
    meta_loc, own_loc, ack,
    right_send, left_send, lane_recv, sib_send, sib_recv, meta_send,
    row_send, row_fwd, row_recv,
):
    rows = x_ref.shape[0]
    half = rows // 2
    chips = STEPS
    sizes = piece_sizes(rows)
    pieces = len(sizes)
    meta = pieces
    i = lax.axis_index("row")
    j = lax.axis_index("col")
    z, c = j // CORES, j % CORES
    y, x = i // 2, i % 2
    xn = 2 * y + (1 - x)
    yn = 2 * (1 - y) + x
    dg = 2 * (1 - y) + (1 - x)
    sib = j + 1 - 2 * c
    right, left = j + CORES, j - CORES
    inner_right = z < chips - 1
    inner_left = z > 0
    tiles = CORES * chips

    barrier = pltpu.get_barrier_semaphore()

    def greet(row, col):
        pl.semaphore_signal(barrier, inc=1, device_id=(row, col), device_id_type=MESH)

    def answer(k, row, col):
        pl.semaphore_signal(ack.at[k], inc=1, device_id=(row, col), device_id_type=MESH)

    greet(i, sib)
    pl.when(inner_right)(lambda: greet(i, right))
    pl.when(x == 0)(lambda: greet(xn, j))
    pl.when(y == 0)(lambda: greet(yn, j))

    own = pltpu.make_async_copy(x_ref.at[:, 0], a_buf.at[j], own_loc.at[0])
    own_b = pltpu.make_async_copy(x_ref.at[:, 0], b_buf.at[i], own_loc.at[1])
    own.start()
    own_b.start()
    oc_down = pltpu.make_async_copy(oc_ref, oc_s, own_loc.at[2])
    oc_down.start()
    own_meta = [
        pltpu.make_async_copy(xc_ref, meta_v.at[slot], own_loc.at[3 + n]) for n, slot in enumerate((j, tiles + i))
    ]
    for copy in own_meta:
        copy.start()
    pl.semaphore_wait(barrier, 1 + jnp.where(inner_left, 1, 0) + x + y)
    pl.when(inner_left)(lambda: answer(0, i, left))
    pl.when(x == 1)(lambda: answer(1, xn, j))
    pl.when(y == 1)(lambda: answer(2, yn, j))

    def part(k):
        return pl.ds(sum(sizes[:k]), sizes[k])

    def there(zs, core, k):
        if k == meta:
            return meta_v.at[CORES * zs + core]
        return a_buf.at[CORES * zs + core, part(k)]

    def here(d, zs, k):
        if d != 0:
            return there(zs, c, k)
        return xc_ref if k == meta else x_ref.at[part(k), 0]

    def to_right(d, zs, k):
        done = meta_send.at[0, d] if k == meta else right_send.at[d]
        return remote(here(d, zs, k), there(zs, c, k), done, lane_recv.at[zs, k], i, right)

    def to_left(d, zs, k):
        done = meta_send.at[1, d] if k == meta else left_send.at[d]
        return remote(here(d, zs, k), there(zs, c, k), done, lane_recv.at[zs, k], i, left)

    def sib_slot(d, k):
        return k if k == meta or d == chips - 1 else 0

    def to_sib(d, zs, k):
        done = meta_send.at[2, zs] if k == meta else sib_send.at[zs]
        return remote(here(d, zs, k), there(zs, c, k), done, sib_recv.at[zs, sib_slot(d, k)], i, sib)

    def lane_wait(zs, k):
        remote(there(zs, c, k), there(zs, c, k), sib_send.at[zs], lane_recv.at[zs, k], i, sib).wait_recv()

    def sib_wait(zs, k):
        mine = there(zs, 1 - c, k)
        remote(mine, mine, sib_send.at[zs], sib_recv.at[zs, k], i, sib).wait_recv()

    def sib_wait_whole(zs):
        mine = a_buf.at[CORES * zs + 1 - c]
        remote(mine, mine, sib_send.at[zs], sib_recv.at[zs, 0], i, sib).wait_recv()

    def sent_whole(sem):
        whole = a_buf.at[0]
        remote(whole, whole, sem, sib_recv.at[0, 0], i, sib).wait_send()

    def b_part(p, k):
        if k == 2:
            return meta_v.at[tiles + p]
        return b_buf.at[p, pl.ds(k * half, half)]

    def row_copy(n, k):
        source = xc_ref if k == 2 else x_ref.at[pl.ds(k * half, half), 0]
        return remote(source, b_part(i, k), row_send.at[n, k], row_recv.at[i, k], (xn, yn)[n], j)

    def row_wait(p, k):
        remote(b_part(p, k), b_part(p, k), row_fwd.at[0], row_recv.at[p, k], xn, j).wait_recv()

    def row_forward(n, k):
        p, to = ((xn, yn), (yn, xn))[n]
        return remote(b_part(p, k), b_part(p, k), row_fwd.at[k], row_recv.at[p, k], to, j)

    forwards = [row_forward(0, 0), row_forward(1, 1), row_forward(0, 2)]

    order = [0, meta, *range(1, pieces)]

    def out_left():
        for k in order:
            to_left(0, z, k).start()

    def out_right():
        pl.semaphore_wait(ack.at[0], 1)
        for k in order:
            to_right(0, z, k).start()

    def out_row(n):
        row_copy(n, 2).start()
        for k in range(2):
            row_copy(n, (k, 1 - k)[n]).start()

    pl.when(inner_left)(out_left)
    to_sib(0, z, meta).start()
    remote(x_ref.at[:, 0], a_buf.at[j], sib_send.at[z], sib_recv.at[z, 0], i, sib).start()
    pl.when(x == 1)(lambda: out_row(0))
    pl.when(y == 1)(lambda: out_row(1))
    pl.when(inner_right)(out_right)

    def late_row(n):
        pl.semaphore_wait(ack.at[1 + n], 1)
        out_row(n)

    pl.when(x == 0)(lambda: late_row(0))
    pl.when(y == 0)(lambda: late_row(1))

    def from_left(d, k):
        lane_wait(z - d, k)
        if d < chips - 1:
            pl.when(inner_right)(lambda: to_right(d, z - d, k).start())
        to_sib(d, z - d, k).start()

    def from_right(d, k):
        lane_wait(z + d, k)
        if d < chips - 1:
            pl.when(inner_left)(lambda: to_left(d, z + d, k).start())
        to_sib(d, z + d, k).start()

    def arrive(d, k):
        pl.when(z - d >= 0)(lambda: from_left(d, k))
        pl.when(z + d <= chips - 1)(lambda: from_right(d, k))

    def arrive_loop(d):
        arrive(d, 0)
        arrive(d, meta)
        for k in range(1, pieces):
            arrive(d, k)

    arrive_loop(1)
    row_wait(xn, 2)
    forwards[2].start()
    row_wait(xn, 0)
    forwards[0].start()
    row_wait(yn, 1)
    forwards[1].start()
    arrive_loop(2)
    row_wait(yn, 2)
    row_wait(dg, 2)
    row_wait(xn, 1)
    row_wait(yn, 0)
    row_wait(dg, 0)
    row_wait(dg, 1)
    own.wait()
    own_b.wait()
    oc_down.wait()
    for copy in own_meta:
        copy.wait()

    first = z // 2
    far = (chips - 1) * (1 - first)

    def near(n):
        return n + first

    def lower(start, count):
        down = pltpu.make_async_copy(meta_v.at[pl.ds(start, count)], meta_s.at[pl.ds(start, count)], meta_loc)
        down.start()
        down.wait()

    for n in range(chips - 1):
        sib_wait(near(n), meta)
    lower(CORES * first, CORES * (chips - 1))
    lower(tiles, chips)

    def operands(m, zs):
        lhs, rhs = [], []
        for h in range(CORES):
            t = CORES * zs + h
            at = h * half + meta_s[t, 0, m]
            block = b_buf[zs, at]
            landing = meta_s[tiles + zs, 0, at]
            zero = jnp.zeros_like(block)
            rhs.append(
                jnp.concatenate([jnp.where(landing == oc_s[o, m], block, zero) for o in range(2)], axis=1)
            )
            lhs.append(a_buf[t, m])
        return lhs, rhs

    def product(m, sources):
        lhs, rhs = [], []
        for zs in sources:
            more = operands(m, zs)
            lhs += more[0]
            rhs += more[1]
        return jnp.dot(
            jnp.concatenate(lhs, axis=1), jnp.concatenate(rhs, axis=0), preferred_element_type=jnp.float32
        )

    for n in range(chips - 1):
        sib_wait_whole(near(n))

    def early(m, carry):
        acc[m] = product(m, [near(n) for n in range(chips - 1)])
        return carry

    lax.fori_loop(0, rows, early, 0)

    is_end = jnp.logical_or(z == 0, z == chips - 1)
    not_end = jnp.logical_not(is_end)

    def far_arrive(k):
        pl.when(z == chips - 1)(lambda: from_left(chips - 1, k))
        pl.when(z == 0)(lambda: from_right(chips - 1, k))

    far_arrive(0)
    far_arrive(meta)

    for d in range(chips - 1):
        go_right = jnp.logical_and(inner_right, z - d >= 0)
        go_left = jnp.logical_and(inner_left, z + d <= chips - 1)
        pl.when(go_right)(lambda d=d: to_right(d, z - d, meta).wait_send())
        pl.when(go_left)(lambda d=d: to_left(d, z + d, meta).wait_send())
        if d < chips - 2:
            pl.when(go_right)(lambda d=d: sent_whole(right_send.at[d]))
            pl.when(go_left)(lambda d=d: sent_whole(left_send.at[d]))
        sent_whole(sib_send.at[near(d)])
        to_sib(1, near(d), meta).wait_send()
    to_sib(1, far, meta).wait_send()
    for k in range(3):
        for n in range(2):
            row_copy(n, k).wait_send()
        forwards[k].wait_send()

    sib_wait(far, meta)
    lower(CORES * far, CORES)
    pl.when(not_end)(lambda: sib_wait_whole(far))

    def late(m, carry):
        total = acc[m] + product(m, [far])
        for o in range(2):
            o_ref[m, o] = total[:, o * 128 : (o + 1) * 128].astype(o_ref.dtype)
        return carry

    for k in range(pieces):
        if k < pieces - 1:
            far_arrive(k + 1)
        pl.when(is_end)(lambda k=k: sib_wait(far, k))
        start = sum(sizes[:k])
        lax.fori_loop(start, start + sizes[k], late, 0, unroll=True)

    d = chips - 2
    pl.when(jnp.logical_and(inner_right, z - d >= 0))(lambda: sent_whole(right_send.at[d]))
    pl.when(jnp.logical_and(inner_left, z + d <= chips - 1))(lambda: sent_whole(left_send.at[d]))
    sent_whole(sib_send.at[far])


def on_four_by_eight(xblocks, xcols, outcols):
    rows, _, size, _ = xblocks.shape
    kept = outcols.shape[1]
    slots = CORES * STEPS + STEPS
    pieces = len(piece_sizes(rows))
    dma = pltpu.SemaphoreType.DMA
    return pl.pallas_call(
        kernel,
        out_shape=jax.ShapeDtypeStruct((rows, kept, size, size), jnp.bfloat16),
        in_specs=[
            pl.BlockSpec(memory_space=pltpu.HBM),
            pl.BlockSpec(memory_space=pltpu.HBM),
            pl.BlockSpec(memory_space=pltpu.HBM),
        ],
        out_specs=pl.BlockSpec(memory_space=pltpu.VMEM),
        scratch_shapes=[
            pltpu.VMEM((CORES * STEPS, rows, size, size), jnp.bfloat16),
            pltpu.VMEM((STEPS, rows, size, size), jnp.bfloat16),
            pltpu.VMEM((rows, size, kept * size), jnp.float32),
            pltpu.VMEM((slots, 1, rows), jnp.int32),
            pltpu.SMEM((slots, 1, rows), jnp.int32),
            pltpu.SMEM((kept, rows), jnp.int32),
            dma,
            dma((5,)),
            pltpu.SemaphoreType.REGULAR((3,)),
            dma((STEPS,)),
            dma((STEPS,)),
            dma((STEPS, pieces + 1)),
            dma((STEPS,)),
            dma((STEPS, pieces + 1)),
            dma((3, STEPS)),
            dma((2, 3)),
            dma((3,)),
            dma((STEPS, 3)),
        ],
        compiler_params=pltpu.CompilerParams(
            collective_id=0, has_side_effects=True, vmem_limit_bytes=32 * 1024 * 1024
        ),
    )(*(pltpu.with_memory_space_constraint(v, pltpu.HBM) for v in (xcols.T, outcols.T, xblocks)))


def solution(mesh):
    in_specs = (P("row", "col", None, None), P("row", "col"), P("row", "col"))
    out_specs = P("row", "col", None, None)
    fits = mesh.shape["row"] == STEPS and mesh.shape["col"] == CORES * STEPS
    body = on_four_by_eight if fits else on_any_mesh
    return jax.shard_map(body, mesh=mesh, in_specs=in_specs, out_specs=out_specs, check_vma=False)
```

```python
import functools

import jax
import jax.numpy as jnp
from jax import lax
from jax.experimental import pallas as pl
from jax.experimental.pallas import tpu as pltpu
from jax.sharding import PartitionSpec as P

STEPS = 4
CORES = 2
MESH = pl.DeviceIdType.MESH
SIZES = (1, 3, 3, 3, 2, 1, 1)
KEPT_AT_END = (1, 2, 3, 4)
ROWS = sum(SIZES)
HALF = ROWS // CORES
PIECES = len(SIZES)
META = PIECES
STARTS = tuple(sum(SIZES[:k]) for k in range(PIECES))
LOW = STARTS[KEPT_AT_END[0]]
HIGH = STARTS[KEPT_AT_END[-1]] + SIZES[KEPT_AT_END[-1]]
MOVED = tuple(k for k in range(PIECES) if k not in KEPT_AT_END)
MOVED_ROWS = tuple(m for k in MOVED for m in range(STARTS[k], STARTS[k] + SIZES[k]))
USED = 3
TILES = CORES * STEPS
RELAYED = (
    tuple(k for k in range(PIECES) if STARTS[k] < HALF),
    tuple(k for k in range(PIECES) if STARTS[k] + SIZES[k] > HALF),
)


def passed_along(value, axis, steps):
    count = lax.axis_size(axis)
    pairs = [(source, (source + steps) % count) for source in range(count)]
    return lax.ppermute(value, axis, pairs)


def broadcast(value, axis, source):
    kept = jnp.where(lax.axis_index(axis) == source, value, 0).astype(value.dtype)
    return lax.psum(kept, axis)


def add_products(total, a_blocks, a_cols, b_blocks, b_cols, targets, offset):
    index = offset + a_cols
    picked = index[:, None] == jnp.arange(b_blocks.shape[0], dtype=jnp.int32)[None, :]
    chosen = jnp.einsum(
        "mr,rbc->mbc", picked.astype(b_blocks.dtype), b_blocks, preferred_element_type=jnp.float32
    ).astype(b_blocks.dtype)
    landing = jnp.sum(jnp.where(picked, b_cols[None, :], 0), axis=1)
    product = jnp.einsum("mab,mbc->mac", a_blocks, chosen, preferred_element_type=jnp.float32)
    weight = (landing[:, None] == targets).astype(jnp.float32)
    return total + weight[:, :, None, None] * product[:, None]


def on_any_mesh(xblocks, xcols, outcols):
    row_count = lax.axis_size("row")
    col_count = lax.axis_size("col")
    per_panel = col_count // row_count
    block_rows = xblocks.shape[0]
    tile_cols = block_rows // per_panel
    block_size = xblocks.shape[2]
    kept = outcols.shape[1]
    row_here = lax.axis_index("row")
    own_blocks = xblocks[:, 0]
    own_cols = xcols[:, 0]
    total = jnp.zeros((block_rows, kept, block_size, block_size), jnp.float32)
    moving = (own_blocks, own_cols)
    for step_no in range(STEPS):
        panel = (row_here + step_no) % row_count
        if step_no > 0:
            moving = passed_along((moving[0], moving[1]), "row", -1)
        for half_no in range(per_panel):
            tile_blocks, tile_cols_ids = (
                broadcast(own_blocks, "col", per_panel * panel + half_no),
                broadcast(own_cols, "col", per_panel * panel + half_no),
            )
            total = add_products(
                total,
                tile_blocks,
                tile_cols_ids,
                moving[0],
                moving[1],
                outcols,
                half_no * tile_cols,
            )
    return total.astype(jnp.bfloat16)


def remote(src, dst, send_sem, recv_sem, row, col):
    return pltpu.make_async_remote_copy(
        src_ref=src,
        dst_ref=dst,
        send_sem=send_sem,
        recv_sem=recv_sem,
        device_id=(row, col),
        device_id_type=MESH,
    )


def kernel(
    xc_ref, oc_ref, x_ref, o_ref,
    a_buf, own_buf, end_buf, xn_0, xn_1, yn_0, yn_1, own_used, xn_used, yn_used, own_dg_used, relayed, dg_used, acc, result,
    meta_v, slot_v, oc_v, meta_s, slot_s, oc_s, oc_out_s,
    local, ack, lane_send, lane_recv, sib_send, sib_recv, meta_send,
    row_send, row_recv, dg_send, dg_recv, tab_send, tab_recv, used_send, used_fwd, used_recv,
    oc_send, oc_recv, out_send, out_recv,
):
    i = lax.axis_index("row")
    j = lax.axis_index("col")
    z, c = j // CORES, j % CORES
    y, x = i // 2, i % 2
    xn = 2 * y + (1 - x)
    yn = 2 * (1 - y) + x
    dg = 2 * (1 - y) + (1 - x)
    groups = (i, xn, yn, dg)
    halves = ((xn_0, xn_1), (yn_0, yn_1))
    used = (xn_used, yn_used, own_dg_used)
    sib = j + 1 - 2 * c
    is_end = jnp.logical_or(z == 0, z == STEPS - 1)
    inner = jnp.logical_not(is_end)
    step = jnp.where(z < STEPS // 2, 1, -1)
    toward = (jnp.where(is_end, j + CORES * step, j - CORES * step), j + CORES * step)
    z_end = jnp.where(is_end, z, z - step)
    z_mid = z + step
    z_far = z + 2 * step
    j_end = CORES * z_end + c

    barrier = pltpu.get_barrier_semaphore()

    def greet(row, col):
        pl.semaphore_signal(barrier, inc=1, device_id=(row, col), device_id_type=MESH)

    def answer(k, row, col):
        pl.semaphore_signal(ack.at[k], inc=1, device_id=(row, col), device_id_type=MESH)

    has_upper = z < STEPS - 1
    has_lower = z > 0
    greet(i, sib)
    pl.when(has_upper)(lambda: greet(i, j + CORES))
    pl.when(x == 0)(lambda: greet(xn, j))
    pl.when(y == 0)(lambda: greet(yn, j))
    own = pltpu.make_async_copy(x_ref.at[:, 0], a_buf.at[j], local.at[0])
    own_again = pltpu.make_async_copy(x_ref.at[:, 0], own_buf, local.at[6])
    own_oc = pltpu.make_async_copy(oc_ref, oc_s, local.at[1])
    own_meta = pltpu.make_async_copy(xc_ref, meta_v.at[TILES * i + j], local.at[2])
    own.start()
    own_again.start()
    own_oc.start()
    own_meta.start()
    pl.semaphore_wait(barrier, 1 + jnp.where(has_lower, 1, 0) + x + y)
    pl.when(has_lower)(lambda: answer(0, i, j - CORES))
    pl.when(x == 1)(lambda: answer(1, xn, j))
    pl.when(y == 1)(lambda: answer(2, yn, j))

    def await_z():
        pl.semaphore_wait(ack.at[0], 1)

    def await_row():
        pl.when(x == 0)(lambda: pl.semaphore_wait(ack.at[1], 1))
        pl.when(y == 0)(lambda: pl.semaphore_wait(ack.at[2], 1))

    def part(k):
        return pl.ds(STARTS[k], SIZES[k])

    def there(zt, core, k):
        if k == META:
            return meta_v.at[TILES * i + CORES * zt + core]
        return a_buf.at[CORES * zt + core, part(k)]

    def mine(k):
        return xc_ref if k == META else x_ref.at[part(k), 0]

    def lane_sem(way, zt, k):
        return meta_send.at[way, zt] if k == META else lane_send.at[way, zt]

    def send_own(way, k):
        remote(mine(k), there(z, c, k), lane_sem(way, z, k), lane_recv.at[z, k], i, toward[way]).start()

    def send_on(way, zt, k):
        here = there(zt, c, k)
        remote(here, here, lane_sem(way, zt, k), lane_recv.at[zt, k], i, toward[way]).start()

    def to_sib(zt, k):
        here = there(zt, c, k)
        done = meta_send.at[2, zt] if k == META else sib_send.at[zt]
        remote(here, here, done, sib_recv.at[zt, k], i, sib).start()

    def lane_wait(zt, k):
        here = there(zt, c, k)
        remote(here, here, sib_send.at[zt], lane_recv.at[zt, k], i, sib).wait_recv()

    def sib_wait(zt, k):
        here = there(zt, 1 - c, k)
        remote(here, here, sib_send.at[zt], sib_recv.at[zt, k], i, sib).wait_recv()

    def sib_wait_whole(zt):
        here = a_buf.at[CORES * zt + 1 - c]
        remote(here, here, sib_send.at[zt], sib_recv.at[zt, 0], i, sib).wait_recv()

    def sent(here, sem):
        remote(here, here, sem, sib_recv.at[0, 0], i, sib).wait_send()

    def own_to_sib():
        remote(xc_ref, there(z, c, META), meta_send.at[2, z], sib_recv.at[z, META], i, sib).start()
        remote(x_ref.at[:, 0], a_buf.at[j], sib_send.at[z], sib_recv.at[z, 0], i, sib).start()

    def row_part(n, k):
        h = STARTS[k] // HALF
        return halves[n][h].at[pl.ds(STARTS[k] - h * HALF, SIZES[k])]

    def to_rows(source, k):
        for n in range(2):
            remote(source, row_part(n, k), row_send.at[n], row_recv.at[n, k], (xn, yn)[n], j).start()

    def row_wait(n, k):
        here = row_part(n, k)
        remote(here, here, row_send.at[n], row_recv.at[n, k], xn, j).wait_recv()

    def dg_on(n):
        for k in RELAYED[n]:
            row_wait(n, k)
        for u in range(USED):
            relayed[n, u] = halves[n][n][slot_s[1, CORES * groups[1 + n] + n, u]]
        remote(relayed.at[n], used_part(dg_used, n), dg_send.at[n], dg_recv.at[n], (yn, xn)[n], j).start()

    def row_rest():
        for n in range(2):
            for k in range(PIECES):
                if k not in RELAYED[n]:
                    row_wait(n, k)
            remote(relayed.at[n], used_part(dg_used, n), dg_send.at[n], dg_recv.at[n], xn, j).wait_recv()

    def rows_sent():
        for n in range(2):
            sent(own_buf, row_send.at[n])
            sent(relayed.at[n], dg_send.at[n])

    def used_part(ref, h):
        return ref.at[pl.ds(h * USED, USED)]

    def table(r):
        return meta_v.at[pl.ds(TILES * r, TILES)]

    def table_out():
        for n in range(2):
            remote(table(i), table(i), tab_send.at[n], tab_recv.at[i], (xn, yn)[n], j).start()

    def table_wait(r):
        remote(table(r), table(r), tab_send.at[0], tab_recv.at[r], xn, j).wait_recv()

    def table_on():
        table_wait(xn)
        remote(table(xn), table(xn), tab_send.at[2], tab_recv.at[xn], yn, j).start()

    def table_rest():
        table_wait(yn)
        table_wait(dg)
        down = pltpu.make_async_copy(meta_v, meta_s, local.at[3])
        down.start()
        return down

    def find_slots():
        values = [
            jnp.concatenate([meta_v[TILES * r + t] for t in range(TILES)], axis=0) for r in range(STEPS)
        ]

        def largest(below):
            best = functools.reduce(
                jnp.maximum, [v if below is None else jnp.where(v < below, v, -1) for v in values]
            )
            best = jnp.max(best, axis=1, keepdims=True)
            return best if below is None else jnp.where(best < 0, below, best)

        high = largest(None)
        middle = largest(high)
        low = largest(middle)
        here = jnp.concatenate([meta_v[TILES * i + t] for t in range(TILES)], axis=0)
        slot_v[0, :, 0:ROWS] = jnp.where(here == high, 2, jnp.where(here == middle, 1, 0))
        lane_id = lax.broadcasted_iota(jnp.int32, (TILES, 128), 1)
        slot_v[1] = jnp.where(lane_id == 0, low, jnp.where(lane_id == 1, middle, high))
        slots_down = pltpu.make_async_copy(slot_v, slot_s, local.at[4])
        slots_down.start()
        slots_down.wait()

    def tables_sent():
        for n in range(3):
            sent(table(i), tab_send.at[n])

    def product(m, tile, pick, targets, which=range(STEPS)):
        lhs, rhs = [], []
        for g in which:
            for h in range(CORES):
                t = CORES * groups[g] + h
                at = h * HALF + meta_s[TILES * i + t, 0, m]
                block = pick(g, h, t, m)
                landing = meta_s[TILES * groups[g] + tile, 0, at]
                zero = jnp.zeros_like(block)
                rhs.append(jnp.concatenate([jnp.where(landing == targets[o, m], block, zero) for o in range(2)], axis=1))
                lhs.append(a_buf[t, m])
        return jnp.dot(
            jnp.concatenate(lhs, axis=1), jnp.concatenate(rhs, axis=0), preferred_element_type=jnp.float32
        )

    def from_whole(first):
        def pick(g, h, t, m):
            if g == STEPS - 1:
                return dg_used[h * USED + slot_s[0, t, m]]
            v = meta_s[TILES * i + t, 0, m]
            return first[h * HALF + v] if g == 0 else halves[g - 1][h][v]

        return pick

    def from_used(g, h, t, m):
        if g == 0:
            return own_buf[h * HALF + meta_s[TILES * i + t, 0, m]]
        return used[g - 1][h * USED + slot_s[0, t, m]]

    def store(ref, at, total):
        for o in range(2):
            ref[at, o] = total[:, o * 128 : (o + 1) * 128].astype(ref.dtype)

    def end_chip():
        z2, z3 = z_far, z + 3 * step

        def out():
            send_own(0, META)
            remote(oc_ref, oc_v, oc_send, oc_recv, i, toward[0]).start()
            for k in range(PIECES):
                send_own(0, k)

        pl.when(has_lower)(out)
        own_to_sib()

        def out_up():
            await_z()
            out()

        pl.when(has_upper)(out_up)
        await_row()
        for k in range(PIECES):
            to_rows(x_ref.at[part(k), 0], k)

        def arrived(zt, k):
            lane_wait(zt, k)
            to_sib(zt, k)

        arrived(z_mid, META)
        for k in KEPT_AT_END[:2]:
            arrived(z_mid, k)
        arrived(z2, META)
        arrived(z3, META)
        own_meta.wait()
        for zt in (z, z_mid, z2, z3):
            sib_wait(zt, META)
        table_out()
        for k in KEPT_AT_END[2:]:
            arrived(z_mid, k)
        table_on()
        down = table_rest()
        own.wait()
        own_again.wait()
        own_oc.wait()
        find_slots()
        dg_on(0)
        dg_on(1)
        for k in KEPT_AT_END:
            arrived(z2, k)
        row_rest()
        sib_wait_whole(z)
        down.wait()
        for k in KEPT_AT_END:
            for zt in (z_mid, z2):
                sib_wait(zt, k)
        for k in KEPT_AT_END:
            arrived(z3, k)
            sib_wait(z3, k)

            def row(m, carry):
                store(o_ref, m, product(m, j, from_whole(own_buf), oc_s))
                return carry

            lax.fori_loop(STARTS[k], STARTS[k] + SIZES[k], row, 0)
        sent(there(z, c, META), meta_send.at[0, z])
        sent(oc_v, oc_send)
        sent(a_buf.at[j], lane_send.at[0, z])
        for zt in (z, z_mid, z2, z3):
            sent(there(zt, c, META), meta_send.at[2, zt])
        sent(a_buf.at[j], sib_send.at[z])
        for zt in (z_mid, z2, z3):
            sent(a_buf.at[j, pl.ds(LOW, HIGH - LOW)], sib_send.at[zt])
        rows_sent()
        tables_sent()
        for k in MOVED:
            here = o_ref.at[part(k)]
            remote(here, here, out_send, out_recv.at[k], i, sib).wait_recv()

    def inner_chip():
        def out_end():
            send_own(0, META)
            for k in KEPT_AT_END:
                send_own(0, k)

        def out_mid():
            for k in (META, 0, KEPT_AT_END[0]):
                send_own(1, k)

        pl.when(z == 1)(out_end)
        pl.when(z == 2)(out_mid)
        own_to_sib()
        await_z()
        pl.when(z == 1)(out_mid)
        pl.when(z == 2)(out_end)
        await_row()

        def from_end(k):
            lane_wait(z_end, k)
            send_on(1, z_end, k)
            if k != META:
                to_rows(a_buf.at[j_end, part(k)], k)
            to_sib(z_end, k)

        def from_mid(zt, k):
            lane_wait(zt, k)
            if k == META or k in KEPT_AT_END:
                send_on(0, zt, k)
            to_sib(zt, k)

        def used_out():
            for h in range(CORES):
                for n in range(USED):
                    own_used[h * USED + n] = own_buf[h * HALF + slot_s[1, CORES * i + h, n]]


            for n in range(2):
                for h in (n, 1 - n):
                    remote(
                        used_part(own_used, h), used_part(used[n], h), used_send.at[n], used_recv.at[n, h],
                        (xn, yn)[n], j,
                    ).start()

        def used_wait(n, h):
            dst = used_part(used[n], h)
            remote(dst, dst, used_fwd.at[0], used_recv.at[n, h], xn, j).wait_recv()

        def used_on(n):
            used_wait(n, n)
            remote(
                used_part(used[n], n), used_part(used[2], n), used_fwd.at[n], used_recv.at[2, n],
                (yn, xn)[n], j,
            ).start()

        def moved(k):
            for zt in (z_end, z_mid, z_far):
                sib_wait(zt, k)
            at = MOVED_ROWS.index(STARTS[k])

            def row(m, carry):
                store(result, m + at, product(m + STARTS[k], j_end, from_whole(end_buf), oc_out_s))
                return carry

            lax.fori_loop(0, SIZES[k], row, 0)
            remote(
                result.at[pl.ds(at, SIZES[k])], o_ref.at[part(k)], out_send, out_recv.at[k], i, toward[0]
            ).start()

        from_end(META)
        from_mid(z_mid, META)
        from_end(0)
        for k in KEPT_AT_END[1:]:
            send_own(1, k)
        from_mid(z_mid, 0)
        from_end(KEPT_AT_END[0])
        from_mid(z_mid, KEPT_AT_END[0])
        from_mid(z_far, META)
        from_end(KEPT_AT_END[1])
        own_meta.wait()
        for zt in (z, z_end, z_mid, z_far):
            sib_wait(zt, META)
        table_out()
        from_mid(z_far, 0)
        from_end(KEPT_AT_END[2])
        from_mid(z_mid, KEPT_AT_END[1])
        table_on()
        for k in KEPT_AT_END[3:]:
            from_end(k)
        from_mid(z_mid, KEPT_AT_END[2])
        for k in MOVED[1:]:
            send_own(1, k)
            from_end(k)
        end_down = pltpu.make_async_copy(a_buf.at[j_end], end_buf, local.at[7])
        end_down.start()
        for k in KEPT_AT_END[3:]:
            from_mid(z_mid, k)
        down = table_rest()
        own.wait()
        own_again.wait()
        find_slots()
        from_mid(z_far, KEPT_AT_END[0])
        dg_on(0)
        from_mid(z_far, KEPT_AT_END[1])
        dg_on(1)
        used_out()
        for k in KEPT_AT_END[2:]:
            from_mid(z_far, k)
        oc_wait = remote(oc_v, oc_v, oc_send, oc_recv, i, sib)
        oc_wait.wait_recv()
        oc_down = pltpu.make_async_copy(oc_v, oc_out_s, local.at[5])
        oc_down.start()
        down.wait()
        own_oc.wait()
        oc_down.wait()
        sib_wait_whole(z)
        row_rest()
        end_down.wait()
        moved(0)
        for k in MOVED[1:]:
            from_mid(z_mid, k)
            from_mid(z_far, k)
        used_on(0)
        used_on(1)
        for k in MOVED[1:]:
            moved(k)
        for k in KEPT_AT_END:
            for zt in (z_end, z_mid, z_far):
                sib_wait(zt, k)
        for n in range(2):
            used_wait(n, 1 - n)

        def early(m, carry):
            acc[m] = product(m, j, from_used, oc_s, range(STEPS - 1))
            return carry

        lax.fori_loop(0, ROWS, early, 0)
        for n in range(2):
            used_wait(2, n)

        def row(m, carry):
            store(o_ref, m, acc[m] + product(m, j, from_used, oc_s, (STEPS - 1,)))
            return carry

        lax.fori_loop(0, ROWS, row, 0)
        for way, zts in enumerate(((z, z_mid, z_far), (z, z_end))):
            for zt in zts:
                sent(there(zt, c, META), meta_send.at[way, zt])
                whole = a_buf.at[0, pl.ds(LOW, HIGH - LOW)] if way == 0 else a_buf.at[0]
                sent(whole, lane_send.at[way, zt])
        for zt in (z, z_end, z_mid, z_far):
            sent(there(zt, c, META), meta_send.at[2, zt])
            sent(a_buf.at[0], sib_send.at[zt])
        rows_sent()
        tables_sent()
        for n in range(2):
            sent(own_used, used_send.at[n])
            sent(used_part(own_used, 0), used_fwd.at[n])
        sent(result, out_send)

    pl.when(inner)(inner_chip)
    pl.when(is_end)(end_chip)


def on_four_by_eight(xblocks, xcols, outcols):
    rows, _, size, _ = xblocks.shape
    kept = outcols.shape[1]
    dma = pltpu.SemaphoreType.DMA
    tile = (rows, size, size)
    return pl.pallas_call(
        kernel,
        out_shape=jax.ShapeDtypeStruct((rows, kept, size, size), jnp.bfloat16),
        in_specs=[pl.BlockSpec(memory_space=pltpu.HBM)] * 3,
        out_specs=pl.BlockSpec(memory_space=pltpu.VMEM),
        scratch_shapes=[
            pltpu.VMEM((TILES, *tile), jnp.bfloat16),
            *[pltpu.VMEM(tile, jnp.bfloat16)] * 2,
            *[pltpu.VMEM((HALF, size, size), jnp.bfloat16)] * 4,
            *[pltpu.VMEM((CORES * USED, size, size), jnp.bfloat16)] * 4,
            pltpu.VMEM((2, USED, size, size), jnp.bfloat16),
            pltpu.VMEM((CORES * USED, size, size), jnp.bfloat16),
            pltpu.VMEM((rows, size, kept * size), jnp.float32),
            pltpu.VMEM((len(MOVED_ROWS), kept, size, size), jnp.bfloat16),
            pltpu.VMEM((STEPS * TILES, 1, rows), jnp.int32),
            pltpu.VMEM((2, TILES, 128), jnp.int32),
            pltpu.VMEM((kept, rows), jnp.int32),
            pltpu.SMEM((STEPS * TILES, 1, rows), jnp.int32),
            pltpu.SMEM((2, TILES, 128), jnp.int32),
            pltpu.SMEM((kept, rows), jnp.int32),
            pltpu.SMEM((kept, rows), jnp.int32),
            dma((8,)),
            pltpu.SemaphoreType.REGULAR((3,)),
            dma((2, STEPS)),
            dma((STEPS, PIECES + 1)),
            dma((STEPS,)),
            dma((STEPS, PIECES + 1)),
            dma((3, STEPS)),
            dma((2,)),
            dma((2, PIECES)),
            dma((2,)),
            dma((2,)),
            dma((3,)),
            dma((STEPS,)),
            dma((2,)),
            dma((2,)),
            dma((3, 2)),
            dma,
            dma,
            dma,
            dma((PIECES,)),
        ],
        compiler_params=pltpu.CompilerParams(
            collective_id=0, has_side_effects=True, vmem_limit_bytes=32 * 1024 * 1024
        ),
    )(*(pltpu.with_memory_space_constraint(v, pltpu.HBM) for v in (xcols.T, outcols.T, xblocks)))


def solution(mesh):
    in_specs = (P("row", "col", None, None), P("row", "col"), P("row", "col"))
    out_specs = P("row", "col", None, None)
    fits = mesh.shape["row"] == STEPS and mesh.shape["col"] == CORES * STEPS
    body = on_four_by_eight if fits else on_any_mesh
    return jax.shard_map(body, mesh=mesh, in_specs=in_specs, out_specs=out_specs, check_vma=False)
```

```python
import functools

import jax
import jax.numpy as jnp
from jax import lax
from jax.experimental import pallas as pl
from jax.experimental.pallas import tpu as pltpu
from jax.sharding import PartitionSpec as P

STEPS = 4
CORES = 2
MESH = pl.DeviceIdType.MESH
SIZES = (1, 3, 3, 3, 2, 1, 1)
KEPT_AT_END = (1, 2, 3, 4)
ROWS = sum(SIZES)
HALF = ROWS // CORES
PIECES = len(SIZES)
META = PIECES
STARTS = tuple(sum(SIZES[:k]) for k in range(PIECES))
LOW = STARTS[KEPT_AT_END[0]]
HIGH = STARTS[KEPT_AT_END[-1]] + SIZES[KEPT_AT_END[-1]]
MOVED = tuple(k for k in range(PIECES) if k not in KEPT_AT_END)
MOVED_ROWS = tuple(m for k in MOVED for m in range(STARTS[k], STARTS[k] + SIZES[k]))
USED = 3
TILES = CORES * STEPS
RELAYED = (
    tuple(k for k in range(PIECES) if STARTS[k] < HALF),
    tuple(k for k in range(PIECES) if STARTS[k] + SIZES[k] > HALF),
)


def passed_along(value, axis, steps):
    count = lax.axis_size(axis)
    pairs = [(source, (source + steps) % count) for source in range(count)]
    return lax.ppermute(value, axis, pairs)


def broadcast(value, axis, source):
    kept = jnp.where(lax.axis_index(axis) == source, value, 0).astype(value.dtype)
    return lax.psum(kept, axis)


def add_products(total, a_blocks, a_cols, b_blocks, b_cols, targets, offset):
    index = offset + a_cols
    picked = index[:, None] == jnp.arange(b_blocks.shape[0], dtype=jnp.int32)[None, :]
    chosen = jnp.einsum(
        "mr,rbc->mbc", picked.astype(b_blocks.dtype), b_blocks, preferred_element_type=jnp.float32
    ).astype(b_blocks.dtype)
    landing = jnp.sum(jnp.where(picked, b_cols[None, :], 0), axis=1)
    product = jnp.einsum("mab,mbc->mac", a_blocks, chosen, preferred_element_type=jnp.float32)
    weight = (landing[:, None] == targets).astype(jnp.float32)
    return total + weight[:, :, None, None] * product[:, None]


def on_any_mesh(xblocks, xcols, outcols):
    row_count = lax.axis_size("row")
    col_count = lax.axis_size("col")
    per_panel = col_count // row_count
    block_rows = xblocks.shape[0]
    tile_cols = block_rows // per_panel
    block_size = xblocks.shape[2]
    kept = outcols.shape[1]
    row_here = lax.axis_index("row")
    own_blocks = xblocks[:, 0]
    own_cols = xcols[:, 0]
    total = jnp.zeros((block_rows, kept, block_size, block_size), jnp.float32)
    moving = (own_blocks, own_cols)
    for step_no in range(STEPS):
        panel = (row_here + step_no) % row_count
        if step_no > 0:
            moving = passed_along((moving[0], moving[1]), "row", -1)
        for half_no in range(per_panel):
            tile_blocks, tile_cols_ids = (
                broadcast(own_blocks, "col", per_panel * panel + half_no),
                broadcast(own_cols, "col", per_panel * panel + half_no),
            )
            total = add_products(
                total,
                tile_blocks,
                tile_cols_ids,
                moving[0],
                moving[1],
                outcols,
                half_no * tile_cols,
            )
    return total.astype(jnp.bfloat16)


def remote(src, dst, send_sem, recv_sem, row, col):
    return pltpu.make_async_remote_copy(
        src_ref=src,
        dst_ref=dst,
        send_sem=send_sem,
        recv_sem=recv_sem,
        device_id=(row, col),
        device_id_type=MESH,
    )


def kernel(
    xc_ref, oc_ref, x_ref, o_ref,
    a_buf, own_buf, end_buf, xn_0, xn_1, yn_0, yn_1, own_used, xn_used, yn_used, own_dg_used, relayed, dg_used, acc, result,
    meta_v, slot_v, oc_v, meta_s, slot_s, oc_s, oc_out_s,
    local, ack, lane_send, lane_recv, sib_send, sib_recv, meta_send,
    row_send, row_recv, dg_send, dg_recv, tab_send, tab_recv, used_send, used_fwd, used_recv,
    oc_send, oc_recv, out_send, out_recv,
):
    i = lax.axis_index("row")
    j = lax.axis_index("col")
    z, c = j // CORES, j % CORES
    y, x = i // 2, i % 2
    xn = 2 * y + (1 - x)
    yn = 2 * (1 - y) + x
    dg = 2 * (1 - y) + (1 - x)
    groups = (i, xn, yn, dg)
    halves = ((xn_0, xn_1), (yn_0, yn_1))
    used = (xn_used, yn_used, own_dg_used)
    sib = j + 1 - 2 * c
    is_end = jnp.logical_or(z == 0, z == STEPS - 1)
    inner = jnp.logical_not(is_end)
    step = jnp.where(z < STEPS // 2, 1, -1)
    toward = (jnp.where(is_end, j + CORES * step, j - CORES * step), j + CORES * step)
    z_end = jnp.where(is_end, z, z - step)
    z_mid = z + step
    z_far = z + 2 * step
    j_end = CORES * z_end + c

    barrier = pltpu.get_barrier_semaphore()

    def greet(row, col):
        pl.semaphore_signal(barrier, inc=1, device_id=(row, col), device_id_type=MESH)

    def answer(k, row, col):
        pl.semaphore_signal(ack.at[k], inc=1, device_id=(row, col), device_id_type=MESH)

    has_upper = z < STEPS - 1
    has_lower = z > 0
    greet(i, sib)
    pl.when(has_upper)(lambda: greet(i, j + CORES))
    pl.when(x == 0)(lambda: greet(xn, j))
    pl.when(y == 0)(lambda: greet(yn, j))
    own = pltpu.make_async_copy(x_ref.at[:, 0], a_buf.at[j], local.at[0])
    own_again = pltpu.make_async_copy(x_ref.at[:, 0], own_buf, local.at[6])
    own_oc = pltpu.make_async_copy(oc_ref, oc_s, local.at[1])
    own_meta = pltpu.make_async_copy(xc_ref, meta_v.at[TILES * i + j], local.at[2])
    own.start()
    own_again.start()
    own_oc.start()
    own_meta.start()
    pl.semaphore_wait(barrier, 1 + jnp.where(has_lower, 1, 0) + x + y)
    pl.when(has_lower)(lambda: answer(0, i, j - CORES))
    pl.when(x == 1)(lambda: answer(1, xn, j))
    pl.when(y == 1)(lambda: answer(2, yn, j))

    def await_z():
        pl.semaphore_wait(ack.at[0], 1)

    def await_row():
        pl.when(x == 0)(lambda: pl.semaphore_wait(ack.at[1], 1))
        pl.when(y == 0)(lambda: pl.semaphore_wait(ack.at[2], 1))

    def part(k):
        return pl.ds(STARTS[k], SIZES[k])

    def there(zt, core, k):
        if k == META:
            return meta_v.at[TILES * i + CORES * zt + core]
        return a_buf.at[CORES * zt + core, part(k)]

    def mine(k):
        return xc_ref if k == META else x_ref.at[part(k), 0]

    def lane_sem(way, zt, k):
        return meta_send.at[way, zt] if k == META else lane_send.at[way, zt]

    def send_own(way, k):
        remote(mine(k), there(z, c, k), lane_sem(way, z, k), lane_recv.at[z, k], i, toward[way]).start()

    def send_on(way, zt, k):
        here = there(zt, c, k)
        remote(here, here, lane_sem(way, zt, k), lane_recv.at[zt, k], i, toward[way]).start()

    def to_sib(zt, k):
        here = there(zt, c, k)
        done = meta_send.at[2, zt] if k == META else sib_send.at[zt]
        remote(here, here, done, sib_recv.at[zt, k], i, sib).start()

    def lane_wait(zt, k):
        here = there(zt, c, k)
        remote(here, here, sib_send.at[zt], lane_recv.at[zt, k], i, sib).wait_recv()

    def sib_wait(zt, k):
        here = there(zt, 1 - c, k)
        remote(here, here, sib_send.at[zt], sib_recv.at[zt, k], i, sib).wait_recv()

    def sib_wait_whole(zt):
        here = a_buf.at[CORES * zt + 1 - c]
        remote(here, here, sib_send.at[zt], sib_recv.at[zt, 0], i, sib).wait_recv()

    def sent(here, sem):
        remote(here, here, sem, sib_recv.at[0, 0], i, sib).wait_send()

    def own_to_sib():
        remote(xc_ref, there(z, c, META), meta_send.at[2, z], sib_recv.at[z, META], i, sib).start()
        remote(x_ref.at[:, 0], a_buf.at[j], sib_send.at[z], sib_recv.at[z, 0], i, sib).start()

    def row_part(n, k):
        h = STARTS[k] // HALF
        return halves[n][h].at[pl.ds(STARTS[k] - h * HALF, SIZES[k])]

    def to_rows(source, k):
        for n in range(2):
            remote(source, row_part(n, k), row_send.at[n], row_recv.at[n, k], (xn, yn)[n], j).start()

    def row_wait(n, k):
        here = row_part(n, k)
        remote(here, here, row_send.at[n], row_recv.at[n, k], xn, j).wait_recv()

    def dg_on(n):
        for k in RELAYED[n]:
            row_wait(n, k)
        for u in range(USED):
            relayed[n, u] = halves[n][n][slot_s[1, CORES * groups[1 + n] + n, u]]
        remote(relayed.at[n], used_part(dg_used, n), dg_send.at[n], dg_recv.at[n], (yn, xn)[n], j).start()

    def row_rest():
        for n in range(2):
            for k in range(PIECES):
                if k not in RELAYED[n]:
                    row_wait(n, k)
            remote(relayed.at[n], used_part(dg_used, n), dg_send.at[n], dg_recv.at[n], xn, j).wait_recv()

    def rows_sent():
        for n in range(2):
            sent(own_buf, row_send.at[n])
            sent(relayed.at[n], dg_send.at[n])

    def used_part(ref, h):
        return ref.at[pl.ds(h * USED, USED)]

    def table(r):
        return meta_v.at[pl.ds(TILES * r, TILES)]

    def table_out():
        for n in range(2):
            remote(table(i), table(i), tab_send.at[n], tab_recv.at[i], (xn, yn)[n], j).start()

    def table_wait(r):
        remote(table(r), table(r), tab_send.at[0], tab_recv.at[r], xn, j).wait_recv()

    def table_on():
        table_wait(xn)
        remote(table(xn), table(xn), tab_send.at[2], tab_recv.at[xn], yn, j).start()

    def table_rest():
        table_wait(yn)
        table_wait(dg)
        down = pltpu.make_async_copy(meta_v, meta_s, local.at[3])
        down.start()
        return down

    def find_slots():
        values = [
            jnp.concatenate([meta_v[TILES * r + t] for t in range(TILES)], axis=0) for r in range(STEPS)
        ]

        def largest(below):
            best = functools.reduce(
                jnp.maximum, [v if below is None else jnp.where(v < below, v, -1) for v in values]
            )
            best = jnp.max(best, axis=1, keepdims=True)
            return best if below is None else jnp.where(best < 0, below, best)

        high = largest(None)
        middle = largest(high)
        low = largest(middle)
        here = jnp.concatenate([meta_v[TILES * i + t] for t in range(TILES)], axis=0)
        slot_v[0, :, 0:ROWS] = jnp.where(here == high, 2, jnp.where(here == middle, 1, 0))
        lane_id = lax.broadcasted_iota(jnp.int32, (TILES, 128), 1)
        slot_v[1] = jnp.where(lane_id == 0, low, jnp.where(lane_id == 1, middle, high))
        slots_down = pltpu.make_async_copy(slot_v, slot_s, local.at[4])
        slots_down.start()
        slots_down.wait()

    def tables_sent():
        for n in range(3):
            sent(table(i), tab_send.at[n])

    def product(m, tile, pick, targets, which=range(STEPS)):
        lhs, rhs = [], []
        for g in which:
            for h in range(CORES):
                t = CORES * groups[g] + h
                at = h * HALF + meta_s[TILES * i + t, 0, m]
                block = pick(g, h, t, m)
                landing = meta_s[TILES * groups[g] + tile, 0, at]
                zero = jnp.zeros_like(block)
                rhs.append(jnp.concatenate([jnp.where(landing == targets[o, m], block, zero) for o in range(2)], axis=1))
                lhs.append(a_buf[t, m])
        return jnp.dot(
            jnp.concatenate(lhs, axis=1), jnp.concatenate(rhs, axis=0), preferred_element_type=jnp.float32
        )

    def from_whole(first):
        def pick(g, h, t, m):
            if g == STEPS - 1:
                return dg_used[h * USED + slot_s[0, t, m]]
            v = meta_s[TILES * i + t, 0, m]
            return first[h * HALF + v] if g == 0 else halves[g - 1][h][v]

        return pick

    def from_used(g, h, t, m):
        if g == 0:
            return own_buf[h * HALF + meta_s[TILES * i + t, 0, m]]
        return used[g - 1][h * USED + slot_s[0, t, m]]

    def store(ref, at, total):
        for o in range(2):
            ref[at, o] = total[:, o * 128 : (o + 1) * 128].astype(ref.dtype)

    def end_chip():
        z2, z3 = z_far, z + 3 * step

        def out():
            send_own(0, META)
            remote(oc_ref, oc_v, oc_send, oc_recv, i, toward[0]).start()
            for k in range(PIECES):
                send_own(0, k)

        pl.when(has_lower)(out)
        own_to_sib()

        def out_up():
            await_z()
            out()

        pl.when(has_upper)(out_up)
        await_row()
        for k in range(PIECES):
            to_rows(x_ref.at[part(k), 0], k)

        def arrived(zt, k):
            lane_wait(zt, k)
            to_sib(zt, k)

        arrived(z_mid, META)
        for k in KEPT_AT_END[:2]:
            arrived(z_mid, k)
        arrived(z2, META)
        arrived(z3, META)
        own_meta.wait()
        for zt in (z, z_mid, z2, z3):
            sib_wait(zt, META)
        table_out()
        for k in KEPT_AT_END[2:]:
            arrived(z_mid, k)
        table_on()
        down = table_rest()
        own.wait()
        own_again.wait()
        own_oc.wait()
        find_slots()
        dg_on(0)
        dg_on(1)
        for k in KEPT_AT_END:
            arrived(z2, k)
        row_rest()
        sib_wait_whole(z)
        down.wait()
        for k in KEPT_AT_END:
            for zt in (z_mid, z2):
                sib_wait(zt, k)
        for k in KEPT_AT_END:
            arrived(z3, k)
            sib_wait(z3, k)

            def row(m, carry):
                store(o_ref, m, product(m, j, from_whole(own_buf), oc_s))
                return carry

            lax.fori_loop(STARTS[k], STARTS[k] + SIZES[k], row, 0, unroll=True)
        sent(there(z, c, META), meta_send.at[0, z])
        sent(oc_v, oc_send)
        sent(a_buf.at[j], lane_send.at[0, z])
        for zt in (z, z_mid, z2, z3):
            sent(there(zt, c, META), meta_send.at[2, zt])
        sent(a_buf.at[j], sib_send.at[z])
        for zt in (z_mid, z2, z3):
            sent(a_buf.at[j, pl.ds(LOW, HIGH - LOW)], sib_send.at[zt])
        rows_sent()
        tables_sent()
        for k in MOVED:
            here = o_ref.at[part(k)]
            remote(here, here, out_send, out_recv.at[k], i, sib).wait_recv()

    def inner_chip():
        def out_end():
            send_own(0, META)
            for k in KEPT_AT_END:
                send_own(0, k)

        def out_mid():
            for k in (META, 0, KEPT_AT_END[0]):
                send_own(1, k)

        pl.when(z == 1)(out_end)
        pl.when(z == 2)(out_mid)
        own_to_sib()
        await_z()
        pl.when(z == 1)(out_mid)
        pl.when(z == 2)(out_end)
        await_row()

        def from_end(k):
            lane_wait(z_end, k)
            send_on(1, z_end, k)
            if k != META:
                to_rows(a_buf.at[j_end, part(k)], k)
            to_sib(z_end, k)

        def from_mid(zt, k):
            lane_wait(zt, k)
            if k == META or k in KEPT_AT_END:
                send_on(0, zt, k)
            to_sib(zt, k)

        def used_out():
            for h in range(CORES):
                for n in range(USED):
                    own_used[h * USED + n] = own_buf[h * HALF + slot_s[1, CORES * i + h, n]]


            for n in range(2):
                for h in (n, 1 - n):
                    remote(
                        used_part(own_used, h), used_part(used[n], h), used_send.at[n], used_recv.at[n, h],
                        (xn, yn)[n], j,
                    ).start()

        def used_wait(n, h):
            dst = used_part(used[n], h)
            remote(dst, dst, used_fwd.at[0], used_recv.at[n, h], xn, j).wait_recv()

        def used_on(n):
            used_wait(n, n)
            remote(
                used_part(used[n], n), used_part(used[2], n), used_fwd.at[n], used_recv.at[2, n],
                (yn, xn)[n], j,
            ).start()

        def moved(k):
            for zt in (z_end, z_mid, z_far):
                sib_wait(zt, k)
            at = MOVED_ROWS.index(STARTS[k])

            def row(m, carry):
                store(result, m + at, product(m + STARTS[k], j_end, from_whole(end_buf), oc_out_s))
                return carry

            lax.fori_loop(0, SIZES[k], row, 0, unroll=True)
            remote(
                result.at[pl.ds(at, SIZES[k])], o_ref.at[part(k)], out_send, out_recv.at[k], i, toward[0]
            ).start()

        from_end(META)
        from_mid(z_mid, META)
        from_end(0)
        for k in KEPT_AT_END[1:]:
            send_own(1, k)
        from_mid(z_mid, 0)
        from_end(KEPT_AT_END[0])
        from_mid(z_mid, KEPT_AT_END[0])
        from_mid(z_far, META)
        own_meta.wait()
        for zt in (z, z_end, z_mid, z_far):
            sib_wait(zt, META)
        table_out()
        from_mid(z_far, 0)
        from_end(KEPT_AT_END[1])
        from_mid(z_mid, KEPT_AT_END[1])
        table_on()
        from_end(KEPT_AT_END[2])
        from_mid(z_mid, KEPT_AT_END[2])
        for k in KEPT_AT_END[3:]:
            from_end(k)
            from_mid(z_mid, k)
        for k in MOVED[1:]:
            send_own(1, k)
            from_end(k)
        end_down = pltpu.make_async_copy(a_buf.at[j_end], end_buf, local.at[7])
        end_down.start()
        down = table_rest()
        own.wait()
        own_again.wait()
        find_slots()
        from_mid(z_far, KEPT_AT_END[0])
        dg_on(0)
        from_mid(z_far, KEPT_AT_END[1])
        dg_on(1)
        used_out()
        for k in KEPT_AT_END[2:]:
            from_mid(z_far, k)
        oc_wait = remote(oc_v, oc_v, oc_send, oc_recv, i, sib)
        oc_wait.wait_recv()
        oc_down = pltpu.make_async_copy(oc_v, oc_out_s, local.at[5])
        oc_down.start()
        down.wait()
        own_oc.wait()
        oc_down.wait()
        sib_wait_whole(z)
        row_rest()
        end_down.wait()
        moved(0)
        for k in MOVED[1:]:
            from_mid(z_mid, k)
            from_mid(z_far, k)
        used_on(0)
        used_on(1)
        for k in MOVED[1:]:
            moved(k)
        for k in KEPT_AT_END:
            for zt in (z_end, z_mid, z_far):
                sib_wait(zt, k)
        for n in range(2):
            used_wait(n, 1 - n)

        def early(m, carry):
            acc[m] = product(m, j, from_used, oc_s, range(STEPS - 1))
            return carry

        lax.fori_loop(0, ROWS, early, 0, unroll=True)
        for n in range(2):
            used_wait(2, n)

        def row(m, carry):
            store(o_ref, m, acc[m] + product(m, j, from_used, oc_s, (STEPS - 1,)))
            return carry

        lax.fori_loop(0, ROWS, row, 0, unroll=True)
        for way, zts in enumerate(((z, z_mid, z_far), (z, z_end))):
            for zt in zts:
                sent(there(zt, c, META), meta_send.at[way, zt])
                whole = a_buf.at[0, pl.ds(LOW, HIGH - LOW)] if way == 0 else a_buf.at[0]
                sent(whole, lane_send.at[way, zt])
        for zt in (z, z_end, z_mid, z_far):
            sent(there(zt, c, META), meta_send.at[2, zt])
            sent(a_buf.at[0], sib_send.at[zt])
        rows_sent()
        tables_sent()
        for n in range(2):
            sent(own_used, used_send.at[n])
            sent(used_part(own_used, 0), used_fwd.at[n])
        sent(result, out_send)

    pl.when(inner)(inner_chip)
    pl.when(is_end)(end_chip)


def on_four_by_eight(xblocks, xcols, outcols):
    rows, _, size, _ = xblocks.shape
    kept = outcols.shape[1]
    dma = pltpu.SemaphoreType.DMA
    tile = (rows, size, size)
    return pl.pallas_call(
        kernel,
        out_shape=jax.ShapeDtypeStruct((rows, kept, size, size), jnp.bfloat16),
        in_specs=[pl.BlockSpec(memory_space=pltpu.HBM)] * 3,
        out_specs=pl.BlockSpec(memory_space=pltpu.VMEM),
        scratch_shapes=[
            pltpu.VMEM((TILES, *tile), jnp.bfloat16),
            *[pltpu.VMEM(tile, jnp.bfloat16)] * 2,
            *[pltpu.VMEM((HALF, size, size), jnp.bfloat16)] * 4,
            *[pltpu.VMEM((CORES * USED, size, size), jnp.bfloat16)] * 4,
            pltpu.VMEM((2, USED, size, size), jnp.bfloat16),
            pltpu.VMEM((CORES * USED, size, size), jnp.bfloat16),
            pltpu.VMEM((rows, size, kept * size), jnp.float32),
            pltpu.VMEM((len(MOVED_ROWS), kept, size, size), jnp.bfloat16),
            pltpu.VMEM((STEPS * TILES, 1, rows), jnp.int32),
            pltpu.VMEM((2, TILES, 128), jnp.int32),
            pltpu.VMEM((kept, rows), jnp.int32),
            pltpu.SMEM((STEPS * TILES, 1, rows), jnp.int32),
            pltpu.SMEM((2, TILES, 128), jnp.int32),
            pltpu.SMEM((kept, rows), jnp.int32),
            pltpu.SMEM((kept, rows), jnp.int32),
            dma((8,)),
            pltpu.SemaphoreType.REGULAR((3,)),
            dma((2, STEPS)),
            dma((STEPS, PIECES + 1)),
            dma((STEPS,)),
            dma((STEPS, PIECES + 1)),
            dma((3, STEPS)),
            dma((2,)),
            dma((2, PIECES)),
            dma((2,)),
            dma((2,)),
            dma((3,)),
            dma((STEPS,)),
            dma((2,)),
            dma((2,)),
            dma((3, 2)),
            dma,
            dma,
            dma,
            dma((PIECES,)),
        ],
        compiler_params=pltpu.CompilerParams(
            collective_id=0, has_side_effects=True, vmem_limit_bytes=32 * 1024 * 1024
        ),
    )(*(pltpu.with_memory_space_constraint(v, pltpu.HBM) for v in (xcols.T, outcols.T, xblocks)))


def solution(mesh):
    in_specs = (P("row", "col", None, None), P("row", "col"), P("row", "col"))
    out_specs = P("row", "col", None, None)
    fits = mesh.shape["row"] == STEPS and mesh.shape["col"] == CORES * STEPS
    body = on_four_by_eight if fits else on_any_mesh
    return jax.shard_map(body, mesh=mesh, in_specs=in_specs, out_specs=out_specs, check_vma=False)
```

```python
import functools

import jax
import jax.numpy as jnp
from jax import lax
from jax.experimental import pallas as pl
from jax.experimental.pallas import tpu as pltpu
from jax.sharding import PartitionSpec as P

STEPS = 4
CORES = 2
MESH = pl.DeviceIdType.MESH
SIZES = (1, 3, 3, 2, 2, 1, 1, 1)
KEPT_AT_END = (1, 2, 3, 4)
ROWS = sum(SIZES)
HALF = ROWS // CORES
PIECES = len(SIZES)
META = PIECES
STARTS = tuple(sum(SIZES[:k]) for k in range(PIECES))
LOW = STARTS[KEPT_AT_END[0]]
HIGH = STARTS[KEPT_AT_END[-1]] + SIZES[KEPT_AT_END[-1]]
MOVED = tuple(k for k in range(PIECES) if k not in KEPT_AT_END)
MOVED_ROWS = tuple(m for k in MOVED for m in range(STARTS[k], STARTS[k] + SIZES[k]))
USED = 3
TILES = CORES * STEPS
RELAYED = (
    tuple(k for k in range(PIECES) if STARTS[k] < HALF),
    tuple(k for k in range(PIECES) if STARTS[k] + SIZES[k] > HALF),
)


def passed_along(value, axis, steps):
    count = lax.axis_size(axis)
    pairs = [(source, (source + steps) % count) for source in range(count)]
    return lax.ppermute(value, axis, pairs)


def broadcast(value, axis, source):
    kept = jnp.where(lax.axis_index(axis) == source, value, 0).astype(value.dtype)
    return lax.psum(kept, axis)


def add_products(total, a_blocks, a_cols, b_blocks, b_cols, targets, offset):
    index = offset + a_cols
    picked = index[:, None] == jnp.arange(b_blocks.shape[0], dtype=jnp.int32)[None, :]
    chosen = jnp.einsum(
        "mr,rbc->mbc", picked.astype(b_blocks.dtype), b_blocks, preferred_element_type=jnp.float32
    ).astype(b_blocks.dtype)
    landing = jnp.sum(jnp.where(picked, b_cols[None, :], 0), axis=1)
    product = jnp.einsum("mab,mbc->mac", a_blocks, chosen, preferred_element_type=jnp.float32)
    weight = (landing[:, None] == targets).astype(jnp.float32)
    return total + weight[:, :, None, None] * product[:, None]


def on_any_mesh(xblocks, xcols, outcols):
    row_count = lax.axis_size("row")
    col_count = lax.axis_size("col")
    per_panel = col_count // row_count
    block_rows = xblocks.shape[0]
    tile_cols = block_rows // per_panel
    block_size = xblocks.shape[2]
    kept = outcols.shape[1]
    row_here = lax.axis_index("row")
    own_blocks = xblocks[:, 0]
    own_cols = xcols[:, 0]
    total = jnp.zeros((block_rows, kept, block_size, block_size), jnp.float32)
    moving = (own_blocks, own_cols)
    for step_no in range(STEPS):
        panel = (row_here + step_no) % row_count
        if step_no > 0:
            moving = passed_along((moving[0], moving[1]), "row", -1)
        for half_no in range(per_panel):
            tile_blocks, tile_cols_ids = (
                broadcast(own_blocks, "col", per_panel * panel + half_no),
                broadcast(own_cols, "col", per_panel * panel + half_no),
            )
            total = add_products(
                total,
                tile_blocks,
                tile_cols_ids,
                moving[0],
                moving[1],
                outcols,
                half_no * tile_cols,
            )
    return total.astype(jnp.bfloat16)


def remote(src, dst, send_sem, recv_sem, row, col):
    return pltpu.make_async_remote_copy(
        src_ref=src,
        dst_ref=dst,
        send_sem=send_sem,
        recv_sem=recv_sem,
        device_id=(row, col),
        device_id_type=MESH,
    )


def kernel(
    xc_ref, oc_ref, x_ref, o_ref,
    a_buf, own_buf, end_buf, xn_0, xn_1, yn_0, yn_1, own_used, xn_used, yn_used, own_dg_used, relayed, dg_used, acc, result,
    meta_v, slot_v, oc_v, meta_s, slot_s, oc_s, oc_out_s,
    local, ack, lane_send, lane_recv, sib_send, sib_recv, meta_send,
    row_send, row_recv, dg_send, dg_recv, tab_send, tab_recv, used_send, used_fwd, used_recv,
    oc_send, oc_recv, out_send, out_recv,
):
    i = lax.axis_index("row")
    j = lax.axis_index("col")
    z, c = j // CORES, j % CORES
    y, x = i // 2, i % 2
    xn = 2 * y + (1 - x)
    yn = 2 * (1 - y) + x
    dg = 2 * (1 - y) + (1 - x)
    groups = (i, xn, yn, dg)
    halves = ((xn_0, xn_1), (yn_0, yn_1))
    used = (xn_used, yn_used, own_dg_used)
    sib = j + 1 - 2 * c
    is_end = jnp.logical_or(z == 0, z == STEPS - 1)
    inner = jnp.logical_not(is_end)
    step = jnp.where(z < STEPS // 2, 1, -1)
    toward = (jnp.where(is_end, j + CORES * step, j - CORES * step), j + CORES * step)
    z_end = jnp.where(is_end, z, z - step)
    z_mid = z + step
    z_far = z + 2 * step
    j_end = CORES * z_end + c

    barrier = pltpu.get_barrier_semaphore()

    def greet(row, col):
        pl.semaphore_signal(barrier, inc=1, device_id=(row, col), device_id_type=MESH)

    def answer(k, row, col):
        pl.semaphore_signal(ack.at[k], inc=1, device_id=(row, col), device_id_type=MESH)

    has_upper = z < STEPS - 1
    has_lower = z > 0
    greet(i, sib)
    pl.when(has_upper)(lambda: greet(i, j + CORES))
    pl.when(x == 0)(lambda: greet(xn, j))
    pl.when(y == 0)(lambda: greet(yn, j))
    own = pltpu.make_async_copy(x_ref.at[:, 0], a_buf.at[j], local.at[0])
    own_again = pltpu.make_async_copy(x_ref.at[:, 0], own_buf, local.at[6])
    own_oc = pltpu.make_async_copy(oc_ref, oc_s, local.at[1])
    own_meta = pltpu.make_async_copy(xc_ref, meta_v.at[TILES * i + j], local.at[2])
    own.start()
    own_again.start()
    own_oc.start()
    own_meta.start()
    pl.semaphore_wait(barrier, 1 + jnp.where(has_lower, 1, 0) + x + y)
    pl.when(has_lower)(lambda: answer(0, i, j - CORES))
    pl.when(x == 1)(lambda: answer(1, xn, j))
    pl.when(y == 1)(lambda: answer(2, yn, j))

    def await_z():
        pl.semaphore_wait(ack.at[0], 1)

    def await_row():
        pl.when(x == 0)(lambda: pl.semaphore_wait(ack.at[1], 1))
        pl.when(y == 0)(lambda: pl.semaphore_wait(ack.at[2], 1))

    def part(k):
        return pl.ds(STARTS[k], SIZES[k])

    def there(zt, core, k):
        if k == META:
            return meta_v.at[TILES * i + CORES * zt + core]
        return a_buf.at[CORES * zt + core, part(k)]

    def mine(k):
        return xc_ref if k == META else x_ref.at[part(k), 0]

    def lane_sem(way, zt, k):
        return meta_send.at[way, zt] if k == META else lane_send.at[way, zt]

    def send_own(way, k):
        remote(mine(k), there(z, c, k), lane_sem(way, z, k), lane_recv.at[z, k], i, toward[way]).start()

    def send_on(way, zt, k):
        here = there(zt, c, k)
        remote(here, here, lane_sem(way, zt, k), lane_recv.at[zt, k], i, toward[way]).start()

    def to_sib(zt, k):
        here = there(zt, c, k)
        done = meta_send.at[2, zt] if k == META else sib_send.at[zt]
        remote(here, here, done, sib_recv.at[zt, k], i, sib).start()

    def lane_wait(zt, k):
        here = there(zt, c, k)
        remote(here, here, sib_send.at[zt], lane_recv.at[zt, k], i, sib).wait_recv()

    def sib_wait(zt, k):
        here = there(zt, 1 - c, k)
        remote(here, here, sib_send.at[zt], sib_recv.at[zt, k], i, sib).wait_recv()

    def sib_wait_whole(zt):
        here = a_buf.at[CORES * zt + 1 - c]
        remote(here, here, sib_send.at[zt], sib_recv.at[zt, 0], i, sib).wait_recv()

    def sent(here, sem):
        remote(here, here, sem, sib_recv.at[0, 0], i, sib).wait_send()

    def own_to_sib():
        remote(xc_ref, there(z, c, META), meta_send.at[2, z], sib_recv.at[z, META], i, sib).start()
        remote(x_ref.at[:, 0], a_buf.at[j], sib_send.at[z], sib_recv.at[z, 0], i, sib).start()

    def row_part(n, k):
        h = STARTS[k] // HALF
        return halves[n][h].at[pl.ds(STARTS[k] - h * HALF, SIZES[k])]

    def to_rows(source, k):
        for n in range(2):
            remote(source, row_part(n, k), row_send.at[n], row_recv.at[n, k], (xn, yn)[n], j).start()

    def row_wait(n, k):
        here = row_part(n, k)
        remote(here, here, row_send.at[n], row_recv.at[n, k], xn, j).wait_recv()

    def dg_on(n):
        for k in RELAYED[n]:
            row_wait(n, k)
        for u in range(USED):
            relayed[n, u] = halves[n][n][slot_s[1, CORES * groups[1 + n] + n, u]]
        remote(relayed.at[n], used_part(dg_used, n), dg_send.at[n], dg_recv.at[n], (yn, xn)[n], j).start()

    def row_rest():
        for n in range(2):
            for k in range(PIECES):
                if k not in RELAYED[n]:
                    row_wait(n, k)
            remote(relayed.at[n], used_part(dg_used, n), dg_send.at[n], dg_recv.at[n], xn, j).wait_recv()

    def rows_sent():
        for n in range(2):
            sent(own_buf, row_send.at[n])
            sent(relayed.at[n], dg_send.at[n])

    def used_part(ref, h):
        return ref.at[pl.ds(h * USED, USED)]

    def table(r):
        return meta_v.at[pl.ds(TILES * r, TILES)]

    def table_out():
        for n in range(2):
            remote(table(i), table(i), tab_send.at[n], tab_recv.at[i], (xn, yn)[n], j).start()

    def table_wait(r):
        remote(table(r), table(r), tab_send.at[0], tab_recv.at[r], xn, j).wait_recv()

    def table_on():
        table_wait(xn)
        remote(table(xn), table(xn), tab_send.at[2], tab_recv.at[xn], yn, j).start()

    def table_rest():
        table_wait(yn)
        table_wait(dg)
        down = pltpu.make_async_copy(meta_v, meta_s, local.at[3])
        down.start()
        return down

    def find_slots():
        values = [
            jnp.concatenate([meta_v[TILES * r + t] for t in range(TILES)], axis=0) for r in range(STEPS)
        ]

        def largest(below):
            best = functools.reduce(
                jnp.maximum, [v if below is None else jnp.where(v < below, v, -1) for v in values]
            )
            best = jnp.max(best, axis=1, keepdims=True)
            return best if below is None else jnp.where(best < 0, below, best)

        high = largest(None)
        middle = largest(high)
        low = largest(middle)
        here = jnp.concatenate([meta_v[TILES * i + t] for t in range(TILES)], axis=0)
        slot_v[0, :, 0:ROWS] = jnp.where(here == high, 2, jnp.where(here == middle, 1, 0))
        lane_id = lax.broadcasted_iota(jnp.int32, (TILES, 128), 1)
        slot_v[1] = jnp.where(lane_id == 0, low, jnp.where(lane_id == 1, middle, high))
        slots_down = pltpu.make_async_copy(slot_v, slot_s, local.at[4])
        slots_down.start()
        slots_down.wait()

    def tables_sent():
        for n in range(3):
            sent(table(i), tab_send.at[n])

    def product(m, tile, pick, targets, which=range(STEPS)):
        lhs, rhs = [], []
        for g in which:
            for h in range(CORES):
                t = CORES * groups[g] + h
                at = h * HALF + meta_s[TILES * i + t, 0, m]
                block = pick(g, h, t, m)
                landing = meta_s[TILES * groups[g] + tile, 0, at]
                zero = jnp.zeros_like(block)
                rhs.append(jnp.concatenate([jnp.where(landing == targets[o, m], block, zero) for o in range(2)], axis=1))
                lhs.append(a_buf[t, m])
        return jnp.dot(
            jnp.concatenate(lhs, axis=1), jnp.concatenate(rhs, axis=0), preferred_element_type=jnp.float32
        )

    def from_whole(first):
        def pick(g, h, t, m):
            if g == STEPS - 1:
                return dg_used[h * USED + slot_s[0, t, m]]
            v = meta_s[TILES * i + t, 0, m]
            return first[h * HALF + v] if g == 0 else halves[g - 1][h][v]

        return pick

    def from_used(g, h, t, m):
        if g == 0:
            return own_buf[h * HALF + meta_s[TILES * i + t, 0, m]]
        return used[g - 1][h * USED + slot_s[0, t, m]]

    def store(ref, at, total):
        for o in range(2):
            ref[at, o] = total[:, o * 128 : (o + 1) * 128].astype(ref.dtype)

    def end_chip():
        z2, z3 = z_far, z + 3 * step

        def out():
            send_own(0, META)
            remote(oc_ref, oc_v, oc_send, oc_recv, i, toward[0]).start()
            for k in range(PIECES):
                send_own(0, k)

        pl.when(has_lower)(out)
        own_to_sib()

        def out_up():
            await_z()
            out()

        pl.when(has_upper)(out_up)
        await_row()
        for k in range(PIECES):
            to_rows(x_ref.at[part(k), 0], k)

        def arrived(zt, k):
            lane_wait(zt, k)
            to_sib(zt, k)

        arrived(z_mid, META)
        for k in KEPT_AT_END[:2]:
            arrived(z_mid, k)
        arrived(z2, META)
        arrived(z3, META)
        own_meta.wait()
        for zt in (z, z_mid, z2, z3):
            sib_wait(zt, META)
        table_out()
        for k in KEPT_AT_END[2:]:
            arrived(z_mid, k)
        table_on()
        down = table_rest()
        own.wait()
        own_again.wait()
        own_oc.wait()
        find_slots()
        dg_on(0)
        dg_on(1)
        for k in KEPT_AT_END:
            arrived(z2, k)
        row_rest()
        sib_wait_whole(z)
        down.wait()
        for k in KEPT_AT_END:
            for zt in (z_mid, z2):
                sib_wait(zt, k)
        for k in KEPT_AT_END:
            arrived(z3, k)
        for k in KEPT_AT_END:
            sib_wait(z3, k)

            def row(m, carry):
                store(o_ref, m, product(m, j, from_whole(own_buf), oc_s))
                return carry

            lax.fori_loop(STARTS[k], STARTS[k] + SIZES[k], row, 0, unroll=True)
        sent(there(z, c, META), meta_send.at[0, z])
        sent(oc_v, oc_send)
        sent(a_buf.at[j], lane_send.at[0, z])
        for zt in (z, z_mid, z2, z3):
            sent(there(zt, c, META), meta_send.at[2, zt])
        sent(a_buf.at[j], sib_send.at[z])
        for zt in (z_mid, z2, z3):
            sent(a_buf.at[j, pl.ds(LOW, HIGH - LOW)], sib_send.at[zt])
        rows_sent()
        tables_sent()
        for k in MOVED:
            here = o_ref.at[part(k)]
            remote(here, here, out_send, out_recv.at[k], i, sib).wait_recv()

    def inner_chip():
        def out_end():
            send_own(0, META)
            for k in KEPT_AT_END[:2]:
                send_own(0, k)

        def out_mid():
            for k in (META, 0, KEPT_AT_END[0]):
                send_own(1, k)

        pl.when(z == 1)(out_end)
        pl.when(z == 2)(out_mid)
        own_to_sib()
        await_z()
        pl.when(z == 1)(out_mid)
        pl.when(z == 2)(out_end)
        await_row()

        def from_end(k):
            lane_wait(z_end, k)
            send_on(1, z_end, k)
            if k != META:
                to_rows(a_buf.at[j_end, part(k)], k)
            to_sib(z_end, k)

        def from_mid(zt, k):
            lane_wait(zt, k)
            if k == META or k in KEPT_AT_END:
                send_on(0, zt, k)
            to_sib(zt, k)

        def used_out():
            for h in range(CORES):
                for n in range(USED):
                    own_used[h * USED + n] = own_buf[h * HALF + slot_s[1, CORES * i + h, n]]


            for n in range(2):
                for h in (n, 1 - n):
                    remote(
                        used_part(own_used, h), used_part(used[n], h), used_send.at[n], used_recv.at[n, h],
                        (xn, yn)[n], j,
                    ).start()

        def used_wait(n, h):
            dst = used_part(used[n], h)
            remote(dst, dst, used_fwd.at[0], used_recv.at[n, h], xn, j).wait_recv()

        def used_on(n):
            used_wait(n, n)
            remote(
                used_part(used[n], n), used_part(used[2], n), used_fwd.at[n], used_recv.at[2, n],
                (yn, xn)[n], j,
            ).start()

        def moved(k):
            for zt in (z_end, z_mid, z_far):
                sib_wait(zt, k)
            at = MOVED_ROWS.index(STARTS[k])

            def row(m, carry):
                store(result, m + at, product(m + STARTS[k], j_end, from_whole(end_buf), oc_out_s))
                return carry

            lax.fori_loop(0, SIZES[k], row, 0, unroll=True)
            remote(
                result.at[pl.ds(at, SIZES[k])], o_ref.at[part(k)], out_send, out_recv.at[k], i, toward[0]
            ).start()

        from_end(META)
        from_mid(z_mid, META)
        send_own(0, KEPT_AT_END[2])
        from_end(0)
        for k in KEPT_AT_END[1:]:
            send_own(1, k)
        from_mid(z_mid, 0)
        from_end(KEPT_AT_END[0])
        from_mid(z_mid, KEPT_AT_END[0])
        from_mid(z_far, META)
        for k in KEPT_AT_END[3:]:
            send_own(0, k)
        own_meta.wait()
        for zt in (z, z_end, z_mid, z_far):
            sib_wait(zt, META)
        table_out()
        from_mid(z_far, 0)
        from_end(KEPT_AT_END[1])
        from_mid(z_mid, KEPT_AT_END[1])
        table_on()
        from_end(KEPT_AT_END[2])
        from_mid(z_mid, KEPT_AT_END[2])
        for k in KEPT_AT_END[3:]:
            from_end(k)
            from_mid(z_mid, k)
        for k in MOVED[1:]:
            send_own(1, k)
            from_end(k)
        end_down = pltpu.make_async_copy(a_buf.at[j_end], end_buf, local.at[7])
        end_down.start()
        down = table_rest()
        own.wait()
        own_again.wait()
        find_slots()
        from_mid(z_far, KEPT_AT_END[0])
        dg_on(0)
        from_mid(z_far, KEPT_AT_END[1])
        dg_on(1)
        used_out()
        for k in KEPT_AT_END[2:]:
            from_mid(z_far, k)
        oc_wait = remote(oc_v, oc_v, oc_send, oc_recv, i, sib)
        oc_wait.wait_recv()
        oc_down = pltpu.make_async_copy(oc_v, oc_out_s, local.at[5])
        oc_down.start()
        down.wait()
        own_oc.wait()
        oc_down.wait()
        sib_wait_whole(z)
        for k in MOVED[1:]:
            from_mid(z_mid, k)
            from_mid(z_far, k)
        row_rest()
        end_down.wait()
        for k in MOVED:
            moved(k)
        used_on(0)
        used_on(1)
        for k in KEPT_AT_END:
            for zt in (z_end, z_mid, z_far):
                sib_wait(zt, k)
        for n in range(2):
            used_wait(n, 1 - n)

        def early(m, carry):
            acc[m] = product(m, j, from_used, oc_s, range(STEPS - 1))
            return carry

        lax.fori_loop(0, ROWS, early, 0, unroll=True)
        for n in range(2):
            used_wait(2, n)

        def row(m, carry):
            store(o_ref, m, acc[m] + product(m, j, from_used, oc_s, (STEPS - 1,)))
            return carry

        lax.fori_loop(0, ROWS, row, 0, unroll=True)
        for way, zts in enumerate(((z, z_mid, z_far), (z, z_end))):
            for zt in zts:
                sent(there(zt, c, META), meta_send.at[way, zt])
                whole = a_buf.at[0, pl.ds(LOW, HIGH - LOW)] if way == 0 else a_buf.at[0]
                sent(whole, lane_send.at[way, zt])
        for zt in (z, z_end, z_mid, z_far):
            sent(there(zt, c, META), meta_send.at[2, zt])
            sent(a_buf.at[0], sib_send.at[zt])
        rows_sent()
        tables_sent()
        for n in range(2):
            sent(own_used, used_send.at[n])
            sent(used_part(own_used, 0), used_fwd.at[n])
        sent(result, out_send)

    pl.when(inner)(inner_chip)
    pl.when(is_end)(end_chip)


def on_four_by_eight(xblocks, xcols, outcols):
    rows, _, size, _ = xblocks.shape
    kept = outcols.shape[1]
    dma = pltpu.SemaphoreType.DMA
    tile = (rows, size, size)
    return pl.pallas_call(
        kernel,
        out_shape=jax.ShapeDtypeStruct((rows, kept, size, size), jnp.bfloat16),
        in_specs=[pl.BlockSpec(memory_space=pltpu.HBM)] * 3,
        out_specs=pl.BlockSpec(memory_space=pltpu.VMEM),
        scratch_shapes=[
            pltpu.VMEM((TILES, *tile), jnp.bfloat16),
            *[pltpu.VMEM(tile, jnp.bfloat16)] * 2,
            *[pltpu.VMEM((HALF, size, size), jnp.bfloat16)] * 4,
            *[pltpu.VMEM((CORES * USED, size, size), jnp.bfloat16)] * 4,
            pltpu.VMEM((2, USED, size, size), jnp.bfloat16),
            pltpu.VMEM((CORES * USED, size, size), jnp.bfloat16),
            pltpu.VMEM((rows, size, kept * size), jnp.float32),
            pltpu.VMEM((len(MOVED_ROWS), kept, size, size), jnp.bfloat16),
            pltpu.VMEM((STEPS * TILES, 1, rows), jnp.int32),
            pltpu.VMEM((2, TILES, 128), jnp.int32),
            pltpu.VMEM((kept, rows), jnp.int32),
            pltpu.SMEM((STEPS * TILES, 1, rows), jnp.int32),
            pltpu.SMEM((2, TILES, 128), jnp.int32),
            pltpu.SMEM((kept, rows), jnp.int32),
            pltpu.SMEM((kept, rows), jnp.int32),
            dma((8,)),
            pltpu.SemaphoreType.REGULAR((3,)),
            dma((2, STEPS)),
            dma((STEPS, PIECES + 1)),
            dma((STEPS,)),
            dma((STEPS, PIECES + 1)),
            dma((3, STEPS)),
            dma((2,)),
            dma((2, PIECES)),
            dma((2,)),
            dma((2,)),
            dma((3,)),
            dma((STEPS,)),
            dma((2,)),
            dma((2,)),
            dma((3, 2)),
            dma,
            dma,
            dma,
            dma((PIECES,)),
        ],
        compiler_params=pltpu.CompilerParams(
            collective_id=0, has_side_effects=True, vmem_limit_bytes=32 * 1024 * 1024
        ),
    )(*(pltpu.with_memory_space_constraint(v, pltpu.HBM) for v in (xcols.T, outcols.T, xblocks)))


def solution(mesh):
    in_specs = (P("row", "col", None, None), P("row", "col"), P("row", "col"))
    out_specs = P("row", "col", None, None)
    fits = mesh.shape["row"] == STEPS and mesh.shape["col"] == CORES * STEPS
    body = on_four_by_eight if fits else on_any_mesh
    return jax.shard_map(body, mesh=mesh, in_specs=in_specs, out_specs=out_specs, check_vma=False)
```

```python
import functools

import jax
import jax.numpy as jnp
from jax import lax
from jax.experimental import pallas as pl
from jax.experimental.pallas import tpu as pltpu
from jax.sharding import PartitionSpec as P

STEPS = 4
CORES = 2
MESH = pl.DeviceIdType.MESH
SIZES = (1, 3, 3, 2, 2, 1, 1, 1)
KEPT_AT_END = (1, 2, 3, 4)
ROWS = sum(SIZES)
HALF = ROWS // CORES
PIECES = len(SIZES)
META = PIECES
STARTS = tuple(sum(SIZES[:k]) for k in range(PIECES))
LOW = STARTS[KEPT_AT_END[0]]
HIGH = STARTS[KEPT_AT_END[-1]] + SIZES[KEPT_AT_END[-1]]
MOVED = tuple(k for k in range(PIECES) if k not in KEPT_AT_END)
MOVED_ROWS = tuple(m for k in MOVED for m in range(STARTS[k], STARTS[k] + SIZES[k]))
USED = 3
TILES = CORES * STEPS
RELAYED = (
    tuple(k for k in range(PIECES) if STARTS[k] < HALF),
    tuple(k for k in range(PIECES) if STARTS[k] + SIZES[k] > HALF),
)


def passed_along(value, axis, steps):
    count = lax.axis_size(axis)
    pairs = [(source, (source + steps) % count) for source in range(count)]
    return lax.ppermute(value, axis, pairs)


def broadcast(value, axis, source):
    kept = jnp.where(lax.axis_index(axis) == source, value, 0).astype(value.dtype)
    return lax.psum(kept, axis)


def add_products(total, a_blocks, a_cols, b_blocks, b_cols, targets, offset):
    index = offset + a_cols
    picked = index[:, None] == jnp.arange(b_blocks.shape[0], dtype=jnp.int32)[None, :]
    chosen = jnp.einsum(
        "mr,rbc->mbc", picked.astype(b_blocks.dtype), b_blocks, preferred_element_type=jnp.float32
    ).astype(b_blocks.dtype)
    landing = jnp.sum(jnp.where(picked, b_cols[None, :], 0), axis=1)
    product = jnp.einsum("mab,mbc->mac", a_blocks, chosen, preferred_element_type=jnp.float32)
    weight = (landing[:, None] == targets).astype(jnp.float32)
    return total + weight[:, :, None, None] * product[:, None]


def on_any_mesh(xblocks, xcols, outcols):
    row_count = lax.axis_size("row")
    col_count = lax.axis_size("col")
    per_panel = col_count // row_count
    block_rows = xblocks.shape[0]
    tile_cols = block_rows // per_panel
    block_size = xblocks.shape[2]
    kept = outcols.shape[1]
    row_here = lax.axis_index("row")
    own_blocks = xblocks[:, 0]
    own_cols = xcols[:, 0]
    total = jnp.zeros((block_rows, kept, block_size, block_size), jnp.float32)
    moving = (own_blocks, own_cols)
    for step_no in range(STEPS):
        panel = (row_here + step_no) % row_count
        if step_no > 0:
            moving = passed_along((moving[0], moving[1]), "row", -1)
        for half_no in range(per_panel):
            tile_blocks, tile_cols_ids = (
                broadcast(own_blocks, "col", per_panel * panel + half_no),
                broadcast(own_cols, "col", per_panel * panel + half_no),
            )
            total = add_products(
                total,
                tile_blocks,
                tile_cols_ids,
                moving[0],
                moving[1],
                outcols,
                half_no * tile_cols,
            )
    return total.astype(jnp.bfloat16)


def remote(src, dst, send_sem, recv_sem, row, col):
    return pltpu.make_async_remote_copy(
        src_ref=src,
        dst_ref=dst,
        send_sem=send_sem,
        recv_sem=recv_sem,
        device_id=(row, col),
        device_id_type=MESH,
    )


def kernel(
    xc_ref, oc_ref, x_ref, o_ref,
    a_buf, own_buf, end_buf, xn_0, xn_1, yn_0, yn_1, own_used, xn_used, yn_used, own_dg_used, relayed, dg_used, acc, result,
    meta_v, slot_v, oc_v, meta_s, slot_s, oc_s, oc_out_s,
    local, ack, lane_send, lane_recv, sib_send, sib_recv, meta_send,
    row_send, row_recv, dg_send, dg_recv, tab_send, tab_recv, used_send, used_fwd, used_recv,
    oc_send, oc_recv, out_send, out_recv,
):
    i = lax.axis_index("row")
    j = lax.axis_index("col")
    z, c = j // CORES, j % CORES
    y, x = i // 2, i % 2
    xn = 2 * y + (1 - x)
    yn = 2 * (1 - y) + x
    dg = 2 * (1 - y) + (1 - x)
    groups = (i, xn, yn, dg)
    halves = ((xn_0, xn_1), (yn_0, yn_1))
    used = (xn_used, yn_used, own_dg_used)
    sib = j + 1 - 2 * c
    is_end = jnp.logical_or(z == 0, z == STEPS - 1)
    inner = jnp.logical_not(is_end)
    step = jnp.where(z < STEPS // 2, 1, -1)
    toward = (jnp.where(is_end, j + CORES * step, j - CORES * step), j + CORES * step)
    z_end = jnp.where(is_end, z, z - step)
    z_mid = z + step
    z_far = z + 2 * step
    j_end = CORES * z_end + c

    barrier = pltpu.get_barrier_semaphore()

    def greet(row, col):
        pl.semaphore_signal(barrier, inc=1, device_id=(row, col), device_id_type=MESH)

    def answer(k, row, col):
        pl.semaphore_signal(ack.at[k], inc=1, device_id=(row, col), device_id_type=MESH)

    has_upper = z < STEPS - 1
    has_lower = z > 0
    greet(i, sib)
    pl.when(has_upper)(lambda: greet(i, j + CORES))
    pl.when(x == 0)(lambda: greet(xn, j))
    pl.when(y == 0)(lambda: greet(yn, j))
    own = pltpu.make_async_copy(x_ref.at[:, 0], a_buf.at[j], local.at[0])
    own_again = pltpu.make_async_copy(x_ref.at[:, 0], own_buf, local.at[6])
    own_oc = pltpu.make_async_copy(oc_ref, oc_s, local.at[1])
    own_meta = pltpu.make_async_copy(xc_ref, meta_v.at[TILES * i + j], local.at[2])
    own.start()
    own_again.start()
    own_oc.start()
    own_meta.start()
    pl.semaphore_wait(barrier, 1 + jnp.where(has_lower, 1, 0) + x + y)
    pl.when(has_lower)(lambda: answer(0, i, j - CORES))
    pl.when(x == 1)(lambda: answer(1, xn, j))
    pl.when(y == 1)(lambda: answer(2, yn, j))

    def await_z():
        pl.semaphore_wait(ack.at[0], 1)

    def await_row():
        pl.when(x == 0)(lambda: pl.semaphore_wait(ack.at[1], 1))
        pl.when(y == 0)(lambda: pl.semaphore_wait(ack.at[2], 1))

    def part(k):
        return pl.ds(STARTS[k], SIZES[k])

    def there(zt, core, k):
        if k == META:
            return meta_v.at[TILES * i + CORES * zt + core]
        return a_buf.at[CORES * zt + core, part(k)]

    def mine(k):
        return xc_ref if k == META else x_ref.at[part(k), 0]

    def lane_sem(way, zt, k):
        return meta_send.at[way, zt] if k == META else lane_send.at[way, zt]

    def send_own(way, k):
        remote(mine(k), there(z, c, k), lane_sem(way, z, k), lane_recv.at[z, k], i, toward[way]).start()

    def send_on(way, zt, k):
        here = there(zt, c, k)
        remote(here, here, lane_sem(way, zt, k), lane_recv.at[zt, k], i, toward[way]).start()

    def to_sib(zt, k):
        here = there(zt, c, k)
        done = meta_send.at[2, zt] if k == META else sib_send.at[zt]
        remote(here, here, done, sib_recv.at[zt, k], i, sib).start()

    def lane_wait(zt, k):
        here = there(zt, c, k)
        remote(here, here, sib_send.at[zt], lane_recv.at[zt, k], i, sib).wait_recv()

    def sib_wait(zt, k):
        here = there(zt, 1 - c, k)
        remote(here, here, sib_send.at[zt], sib_recv.at[zt, k], i, sib).wait_recv()

    def sib_wait_whole(zt):
        here = a_buf.at[CORES * zt + 1 - c]
        remote(here, here, sib_send.at[zt], sib_recv.at[zt, 0], i, sib).wait_recv()

    def sent(here, sem):
        remote(here, here, sem, sib_recv.at[0, 0], i, sib).wait_send()

    def own_to_sib():
        remote(xc_ref, there(z, c, META), meta_send.at[2, z], sib_recv.at[z, META], i, sib).start()
        remote(x_ref.at[:, 0], a_buf.at[j], sib_send.at[z], sib_recv.at[z, 0], i, sib).start()

    def row_part(n, k):
        h = STARTS[k] // HALF
        return halves[n][h].at[pl.ds(STARTS[k] - h * HALF, SIZES[k])]

    def to_rows(source, k):
        for n in range(2):
            remote(source, row_part(n, k), row_send.at[n], row_recv.at[n, k], (xn, yn)[n], j).start()

    def row_wait(n, k):
        here = row_part(n, k)
        remote(here, here, row_send.at[n], row_recv.at[n, k], xn, j).wait_recv()

    def dg_on(n):
        for k in RELAYED[n]:
            row_wait(n, k)
        for u in range(USED):
            relayed[n, u] = halves[n][n][slot_s[1, CORES * groups[1 + n] + n, u]]
        remote(relayed.at[n], used_part(dg_used, n), dg_send.at[n], dg_recv.at[n], (yn, xn)[n], j).start()

    def row_rest():
        for n in range(2):
            for k in range(PIECES):
                if k not in RELAYED[n]:
                    row_wait(n, k)
            remote(relayed.at[n], used_part(dg_used, n), dg_send.at[n], dg_recv.at[n], xn, j).wait_recv()

    def rows_sent():
        for n in range(2):
            sent(own_buf, row_send.at[n])
            sent(relayed.at[n], dg_send.at[n])

    def used_part(ref, h):
        return ref.at[pl.ds(h * USED, USED)]

    def table(r):
        return meta_v.at[pl.ds(TILES * r, TILES)]

    def table_out():
        for n in range(2):
            remote(table(i), table(i), tab_send.at[n], tab_recv.at[i], (xn, yn)[n], j).start()

    def table_wait(r):
        remote(table(r), table(r), tab_send.at[0], tab_recv.at[r], xn, j).wait_recv()

    def table_on():
        table_wait(xn)
        remote(table(xn), table(xn), tab_send.at[2], tab_recv.at[xn], yn, j).start()

    def table_rest():
        table_wait(yn)
        table_wait(dg)
        down = pltpu.make_async_copy(meta_v, meta_s, local.at[3])
        down.start()
        return down

    def find_slots():
        values = [
            jnp.concatenate([meta_v[TILES * r + t] for t in range(TILES)], axis=0) for r in range(STEPS)
        ]

        def largest(below):
            best = functools.reduce(
                jnp.maximum, [v if below is None else jnp.where(v < below, v, -1) for v in values]
            )
            best = jnp.max(best, axis=1, keepdims=True)
            return best if below is None else jnp.where(best < 0, below, best)

        high = largest(None)
        middle = largest(high)
        low = largest(middle)
        here = jnp.concatenate([meta_v[TILES * i + t] for t in range(TILES)], axis=0)
        slot_v[0, :, 0:ROWS] = jnp.where(here == high, 2, jnp.where(here == middle, 1, 0))
        lane_id = lax.broadcasted_iota(jnp.int32, (TILES, 128), 1)
        slot_v[1] = jnp.where(lane_id == 0, low, jnp.where(lane_id == 1, middle, high))
        slots_down = pltpu.make_async_copy(slot_v, slot_s, local.at[4])
        slots_down.start()
        slots_down.wait()

    def tables_sent():
        for n in range(3):
            sent(table(i), tab_send.at[n])

    def product(m, tile, pick, targets, which=range(STEPS)):
        lhs, rhs = [], []
        for g in which:
            for h in range(CORES):
                t = CORES * groups[g] + h
                at = h * HALF + meta_s[TILES * i + t, 0, m]
                block = pick(g, h, t, m)
                landing = meta_s[TILES * groups[g] + tile, 0, at]
                zero = jnp.zeros_like(block)
                rhs.append(jnp.concatenate([jnp.where(landing == targets[o, m], block, zero) for o in range(2)], axis=1))
                lhs.append(a_buf[t, m])
        return jnp.dot(
            jnp.concatenate(lhs, axis=1), jnp.concatenate(rhs, axis=0), preferred_element_type=jnp.float32
        )

    def from_whole(first):
        def pick(g, h, t, m):
            if g == STEPS - 1:
                return dg_used[h * USED + slot_s[0, t, m]]
            v = meta_s[TILES * i + t, 0, m]
            return first[h * HALF + v] if g == 0 else halves[g - 1][h][v]

        return pick

    def from_used(g, h, t, m):
        if g == 0:
            return own_buf[h * HALF + meta_s[TILES * i + t, 0, m]]
        return used[g - 1][h * USED + slot_s[0, t, m]]

    def store(ref, at, total):
        for o in range(2):
            ref[at, o] = total[:, o * 128 : (o + 1) * 128].astype(ref.dtype)

    def end_chip():
        z2, z3 = z_far, z + 3 * step

        def out():
            send_own(0, META)
            remote(oc_ref, oc_v, oc_send, oc_recv, i, toward[0]).start()
            for k in range(PIECES):
                send_own(0, k)

        pl.when(has_lower)(out)
        own_to_sib()

        def out_up():
            await_z()
            out()

        pl.when(has_upper)(out_up)
        await_row()
        for k in range(PIECES):
            to_rows(x_ref.at[part(k), 0], k)

        def arrived(zt, k):
            lane_wait(zt, k)
            to_sib(zt, k)

        arrived(z_mid, META)
        for k in KEPT_AT_END[:2]:
            arrived(z_mid, k)
        arrived(z2, META)
        arrived(z3, META)
        own_meta.wait()
        for zt in (z, z_mid, z2, z3):
            sib_wait(zt, META)
        table_out()
        for k in KEPT_AT_END[2:]:
            arrived(z_mid, k)
        table_on()
        down = table_rest()
        own.wait()
        own_again.wait()
        own_oc.wait()
        find_slots()
        dg_on(0)
        dg_on(1)
        for k in KEPT_AT_END:
            arrived(z2, k)
        row_rest()
        sib_wait_whole(z)
        down.wait()
        for k in KEPT_AT_END:
            for zt in (z_mid, z2):
                sib_wait(zt, k)
        for k in KEPT_AT_END:
            arrived(z3, k)
        for k in KEPT_AT_END:
            sib_wait(z3, k)

            def row(m, carry):
                store(o_ref, m, product(m, j, from_whole(own_buf), oc_s))
                return carry

            lax.fori_loop(STARTS[k], STARTS[k] + SIZES[k], row, 0, unroll=True)
        sent(there(z, c, META), meta_send.at[0, z])
        sent(oc_v, oc_send)
        sent(a_buf.at[j], lane_send.at[0, z])
        for zt in (z, z_mid, z2, z3):
            sent(there(zt, c, META), meta_send.at[2, zt])
        sent(a_buf.at[j], sib_send.at[z])
        for zt in (z_mid, z2, z3):
            sent(a_buf.at[j, pl.ds(LOW, HIGH - LOW)], sib_send.at[zt])
        rows_sent()
        tables_sent()
        for k in MOVED:
            here = o_ref.at[part(k)]
            remote(here, here, out_send, out_recv.at[k], i, sib).wait_recv()

    def inner_chip():
        def out_end():
            send_own(0, META)
            for k in KEPT_AT_END[:2]:
                send_own(0, k)

        def out_mid():
            for k in (META, 0, KEPT_AT_END[0]):
                send_own(1, k)

        pl.when(z == 1)(out_end)
        pl.when(z == 2)(out_mid)
        own_to_sib()
        await_z()
        pl.when(z == 1)(out_mid)
        pl.when(z == 2)(out_end)
        await_row()

        def from_end(k):
            lane_wait(z_end, k)
            if k != META:
                to_rows(a_buf.at[j_end, part(k)], k)
            send_on(1, z_end, k)
            to_sib(z_end, k)

        def from_mid(zt, k):
            lane_wait(zt, k)
            if k == META or k in KEPT_AT_END:
                send_on(0, zt, k)
            to_sib(zt, k)

        def used_out():
            for h in range(CORES):
                for n in range(USED):
                    own_used[h * USED + n] = own_buf[h * HALF + slot_s[1, CORES * i + h, n]]


            for n in range(2):
                for h in (n, 1 - n):
                    remote(
                        used_part(own_used, h), used_part(used[n], h), used_send.at[n], used_recv.at[n, h],
                        (xn, yn)[n], j,
                    ).start()

        def used_wait(n, h):
            dst = used_part(used[n], h)
            remote(dst, dst, used_fwd.at[0], used_recv.at[n, h], xn, j).wait_recv()

        def used_on(n):
            used_wait(n, n)
            remote(
                used_part(used[n], n), used_part(used[2], n), used_fwd.at[n], used_recv.at[2, n],
                (yn, xn)[n], j,
            ).start()

        def moved(k):
            for zt in (z_end, z_mid, z_far):
                sib_wait(zt, k)
            at = MOVED_ROWS.index(STARTS[k])

            def row(m, carry):
                store(result, m + at, product(m + STARTS[k], j_end, from_whole(end_buf), oc_out_s))
                return carry

            lax.fori_loop(0, SIZES[k], row, 0, unroll=True)
            remote(
                result.at[pl.ds(at, SIZES[k])], o_ref.at[part(k)], out_send, out_recv.at[k], i, toward[0]
            ).start()

        from_end(META)
        from_mid(z_mid, META)
        send_own(0, KEPT_AT_END[2])
        from_end(0)
        for k in KEPT_AT_END[1:]:
            send_own(1, k)
        from_mid(z_mid, 0)
        from_end(KEPT_AT_END[0])
        from_mid(z_mid, KEPT_AT_END[0])
        from_mid(z_far, META)
        for k in KEPT_AT_END[3:]:
            send_own(0, k)
        own_meta.wait()
        for zt in (z, z_end, z_mid, z_far):
            sib_wait(zt, META)
        table_out()
        from_mid(z_far, 0)
        from_end(KEPT_AT_END[1])
        from_mid(z_mid, KEPT_AT_END[1])
        table_on()
        from_end(KEPT_AT_END[2])
        from_mid(z_mid, KEPT_AT_END[2])
        for k in KEPT_AT_END[3:]:
            from_end(k)
            from_mid(z_mid, k)
        for k in MOVED[1:]:
            send_own(1, k)
            from_end(k)
        end_down = pltpu.make_async_copy(a_buf.at[j_end], end_buf, local.at[7])
        end_down.start()
        down = table_rest()
        own.wait()
        own_again.wait()
        find_slots()
        from_mid(z_far, KEPT_AT_END[0])
        dg_on(0)
        from_mid(z_far, KEPT_AT_END[1])
        dg_on(1)
        used_out()
        for k in KEPT_AT_END[2:]:
            from_mid(z_far, k)
        oc_wait = remote(oc_v, oc_v, oc_send, oc_recv, i, sib)
        oc_wait.wait_recv()
        oc_down = pltpu.make_async_copy(oc_v, oc_out_s, local.at[5])
        oc_down.start()
        down.wait()
        own_oc.wait()
        oc_down.wait()
        sib_wait_whole(z)
        for k in MOVED[1:]:
            from_mid(z_mid, k)
            from_mid(z_far, k)
        row_rest()
        end_down.wait()
        for k in MOVED:
            moved(k)
        used_on(0)
        used_on(1)
        for k in KEPT_AT_END:
            for zt in (z_end, z_mid, z_far):
                sib_wait(zt, k)
        for n in range(2):
            used_wait(n, 1 - n)

        def early(m, carry):
            acc[m] = product(m, j, from_used, oc_s, range(STEPS - 1))
            return carry

        lax.fori_loop(0, ROWS, early, 0, unroll=True)
        for n in range(2):
            used_wait(2, n)

        def row(m, carry):
            store(o_ref, m, acc[m] + product(m, j, from_used, oc_s, (STEPS - 1,)))
            return carry

        lax.fori_loop(0, ROWS, row, 0, unroll=True)
        for way, zts in enumerate(((z, z_mid, z_far), (z, z_end))):
            for zt in zts:
                sent(there(zt, c, META), meta_send.at[way, zt])
                whole = a_buf.at[0, pl.ds(LOW, HIGH - LOW)] if way == 0 else a_buf.at[0]
                sent(whole, lane_send.at[way, zt])
        for zt in (z, z_end, z_mid, z_far):
            sent(there(zt, c, META), meta_send.at[2, zt])
            sent(a_buf.at[0], sib_send.at[zt])
        rows_sent()
        tables_sent()
        for n in range(2):
            sent(own_used, used_send.at[n])
            sent(used_part(own_used, 0), used_fwd.at[n])
        sent(result, out_send)

    pl.when(inner)(inner_chip)
    pl.when(is_end)(end_chip)


def on_four_by_eight(xblocks, xcols, outcols):
    rows, _, size, _ = xblocks.shape
    kept = outcols.shape[1]
    dma = pltpu.SemaphoreType.DMA
    tile = (rows, size, size)
    return pl.pallas_call(
        kernel,
        out_shape=jax.ShapeDtypeStruct((rows, kept, size, size), jnp.bfloat16),
        in_specs=[pl.BlockSpec(memory_space=pltpu.HBM)] * 3,
        out_specs=pl.BlockSpec(memory_space=pltpu.VMEM),
        scratch_shapes=[
            pltpu.VMEM((TILES, *tile), jnp.bfloat16),
            *[pltpu.VMEM(tile, jnp.bfloat16)] * 2,
            *[pltpu.VMEM((HALF, size, size), jnp.bfloat16)] * 4,
            *[pltpu.VMEM((CORES * USED, size, size), jnp.bfloat16)] * 4,
            pltpu.VMEM((2, USED, size, size), jnp.bfloat16),
            pltpu.VMEM((CORES * USED, size, size), jnp.bfloat16),
            pltpu.VMEM((rows, size, kept * size), jnp.float32),
            pltpu.VMEM((len(MOVED_ROWS), kept, size, size), jnp.bfloat16),
            pltpu.VMEM((STEPS * TILES, 1, rows), jnp.int32),
            pltpu.VMEM((2, TILES, 128), jnp.int32),
            pltpu.VMEM((kept, rows), jnp.int32),
            pltpu.SMEM((STEPS * TILES, 1, rows), jnp.int32),
            pltpu.SMEM((2, TILES, 128), jnp.int32),
            pltpu.SMEM((kept, rows), jnp.int32),
            pltpu.SMEM((kept, rows), jnp.int32),
            dma((8,)),
            pltpu.SemaphoreType.REGULAR((3,)),
            dma((2, STEPS)),
            dma((STEPS, PIECES + 1)),
            dma((STEPS,)),
            dma((STEPS, PIECES + 1)),
            dma((3, STEPS)),
            dma((2,)),
            dma((2, PIECES)),
            dma((2,)),
            dma((2,)),
            dma((3,)),
            dma((STEPS,)),
            dma((2,)),
            dma((2,)),
            dma((3, 2)),
            dma,
            dma,
            dma,
            dma((PIECES,)),
        ],
        compiler_params=pltpu.CompilerParams(
            collective_id=0, has_side_effects=True, vmem_limit_bytes=32 * 1024 * 1024
        ),
    )(*(pltpu.with_memory_space_constraint(v, pltpu.HBM) for v in (xcols.T, outcols.T, xblocks)))


def solution(mesh):
    in_specs = (P("row", "col", None, None), P("row", "col"), P("row", "col"))
    out_specs = P("row", "col", None, None)
    fits = mesh.shape["row"] == STEPS and mesh.shape["col"] == CORES * STEPS
    body = on_four_by_eight if fits else on_any_mesh
    return jax.shard_map(body, mesh=mesh, in_specs=in_specs, out_specs=out_specs, check_vma=False)
```

```python
import functools

import jax
import jax.numpy as jnp
from jax import lax
from jax.experimental import pallas as pl
from jax.experimental.pallas import tpu as pltpu
from jax.sharding import PartitionSpec as P

STEPS = 4
CORES = 2
MESH = pl.DeviceIdType.MESH
SIZES = (1, 2, 4, 3, 2, 1, 1)
KEPT_AT_END = (1, 2, 3, 4)
ROWS = sum(SIZES)
HALF = ROWS // CORES
PIECES = len(SIZES)
META = PIECES
STARTS = tuple(sum(SIZES[:k]) for k in range(PIECES))
LOW = STARTS[KEPT_AT_END[0]]
HIGH = STARTS[KEPT_AT_END[-1]] + SIZES[KEPT_AT_END[-1]]
MOVED = tuple(k for k in range(PIECES) if k not in KEPT_AT_END)
MOVED_ROWS = tuple(m for k in MOVED for m in range(STARTS[k], STARTS[k] + SIZES[k]))
USED = 3
TILES = CORES * STEPS
RELAYED = (
    tuple(k for k in range(PIECES) if STARTS[k] < HALF),
    tuple(k for k in range(PIECES) if STARTS[k] + SIZES[k] > HALF),
)


def passed_along(value, axis, steps):
    count = lax.axis_size(axis)
    pairs = [(source, (source + steps) % count) for source in range(count)]
    return lax.ppermute(value, axis, pairs)


def broadcast(value, axis, source):
    kept = jnp.where(lax.axis_index(axis) == source, value, 0).astype(value.dtype)
    return lax.psum(kept, axis)


def add_products(total, a_blocks, a_cols, b_blocks, b_cols, targets, offset):
    index = offset + a_cols
    picked = index[:, None] == jnp.arange(b_blocks.shape[0], dtype=jnp.int32)[None, :]
    chosen = jnp.einsum(
        "mr,rbc->mbc", picked.astype(b_blocks.dtype), b_blocks, preferred_element_type=jnp.float32
    ).astype(b_blocks.dtype)
    landing = jnp.sum(jnp.where(picked, b_cols[None, :], 0), axis=1)
    product = jnp.einsum("mab,mbc->mac", a_blocks, chosen, preferred_element_type=jnp.float32)
    weight = (landing[:, None] == targets).astype(jnp.float32)
    return total + weight[:, :, None, None] * product[:, None]


def on_any_mesh(xblocks, xcols, outcols):
    row_count = lax.axis_size("row")
    col_count = lax.axis_size("col")
    per_panel = col_count // row_count
    block_rows = xblocks.shape[0]
    tile_cols = block_rows // per_panel
    block_size = xblocks.shape[2]
    kept = outcols.shape[1]
    row_here = lax.axis_index("row")
    own_blocks = xblocks[:, 0]
    own_cols = xcols[:, 0]
    total = jnp.zeros((block_rows, kept, block_size, block_size), jnp.float32)
    moving = (own_blocks, own_cols)
    for step_no in range(STEPS):
        panel = (row_here + step_no) % row_count
        if step_no > 0:
            moving = passed_along((moving[0], moving[1]), "row", -1)
        for half_no in range(per_panel):
            tile_blocks, tile_cols_ids = (
                broadcast(own_blocks, "col", per_panel * panel + half_no),
                broadcast(own_cols, "col", per_panel * panel + half_no),
            )
            total = add_products(
                total,
                tile_blocks,
                tile_cols_ids,
                moving[0],
                moving[1],
                outcols,
                half_no * tile_cols,
            )
    return total.astype(jnp.bfloat16)


def remote(src, dst, send_sem, recv_sem, row, col):
    return pltpu.make_async_remote_copy(
        src_ref=src,
        dst_ref=dst,
        send_sem=send_sem,
        recv_sem=recv_sem,
        device_id=(row, col),
        device_id_type=MESH,
    )


def kernel(
    xc_ref, oc_ref, x_ref, o_ref,
    a_buf, own_buf, end_buf, xn_0, xn_1, yn_0, yn_1, own_used, xn_used, yn_used, own_dg_used, relayed, dg_used, acc, result,
    meta_v, slot_v, oc_v, meta_s, slot_s, oc_s, oc_out_s,
    local, ack, lane_send, lane_recv, sib_send, sib_recv, meta_send,
    row_send, row_recv, dg_send, dg_recv, tab_send, tab_recv, used_send, used_fwd, used_recv,
    oc_send, oc_recv, out_send, out_recv,
):
    i = lax.axis_index("row")
    j = lax.axis_index("col")
    z, c = j // CORES, j % CORES
    y, x = i // 2, i % 2
    xn = 2 * y + (1 - x)
    yn = 2 * (1 - y) + x
    dg = 2 * (1 - y) + (1 - x)
    groups = (i, xn, yn, dg)
    halves = ((xn_0, xn_1), (yn_0, yn_1))
    used = (xn_used, yn_used, own_dg_used)
    sib = j + 1 - 2 * c
    is_end = jnp.logical_or(z == 0, z == STEPS - 1)
    inner = jnp.logical_not(is_end)
    step = jnp.where(z < STEPS // 2, 1, -1)
    toward = (jnp.where(is_end, j + CORES * step, j - CORES * step), j + CORES * step)
    z_end = jnp.where(is_end, z, z - step)
    z_mid = z + step
    z_far = z + 2 * step
    j_end = CORES * z_end + c

    barrier = pltpu.get_barrier_semaphore()

    def greet(row, col):
        pl.semaphore_signal(barrier, inc=1, device_id=(row, col), device_id_type=MESH)

    def answer(k, row, col):
        pl.semaphore_signal(ack.at[k], inc=1, device_id=(row, col), device_id_type=MESH)

    has_upper = z < STEPS - 1
    has_lower = z > 0
    greet(i, sib)
    pl.when(has_upper)(lambda: greet(i, j + CORES))
    pl.when(x == 0)(lambda: greet(xn, j))
    pl.when(y == 0)(lambda: greet(yn, j))
    own = pltpu.make_async_copy(x_ref.at[:, 0], a_buf.at[j], local.at[0])
    own_again = pltpu.make_async_copy(x_ref.at[:, 0], own_buf, local.at[6])
    own_oc = pltpu.make_async_copy(oc_ref, oc_s, local.at[1])
    own_meta = pltpu.make_async_copy(xc_ref, meta_v.at[TILES * i + j], local.at[2])
    own.start()
    own_again.start()
    own_oc.start()
    own_meta.start()
    pl.semaphore_wait(barrier, 1 + jnp.where(has_lower, 1, 0) + x + y)
    pl.when(has_lower)(lambda: answer(0, i, j - CORES))
    pl.when(x == 1)(lambda: answer(1, xn, j))
    pl.when(y == 1)(lambda: answer(2, yn, j))

    def await_z():
        pl.semaphore_wait(ack.at[0], 1)

    def await_row():
        pl.when(x == 0)(lambda: pl.semaphore_wait(ack.at[1], 1))
        pl.when(y == 0)(lambda: pl.semaphore_wait(ack.at[2], 1))

    def part(k):
        return pl.ds(STARTS[k], SIZES[k])

    def there(zt, core, k):
        if k == META:
            return meta_v.at[TILES * i + CORES * zt + core]
        return a_buf.at[CORES * zt + core, part(k)]

    def mine(k):
        return xc_ref if k == META else x_ref.at[part(k), 0]

    def lane_sem(way, zt, k):
        return meta_send.at[way, zt] if k == META else lane_send.at[way, zt]

    def send_own(way, k):
        remote(mine(k), there(z, c, k), lane_sem(way, z, k), lane_recv.at[z, k], i, toward[way]).start()

    def send_on(way, zt, k):
        here = there(zt, c, k)
        remote(here, here, lane_sem(way, zt, k), lane_recv.at[zt, k], i, toward[way]).start()

    def to_sib(zt, k):
        here = there(zt, c, k)
        done = meta_send.at[2, zt] if k == META else sib_send.at[zt]
        remote(here, here, done, sib_recv.at[zt, k], i, sib).start()

    def lane_wait(zt, k):
        here = there(zt, c, k)
        remote(here, here, sib_send.at[zt], lane_recv.at[zt, k], i, sib).wait_recv()

    def sib_wait(zt, k):
        here = there(zt, 1 - c, k)
        remote(here, here, sib_send.at[zt], sib_recv.at[zt, k], i, sib).wait_recv()

    def sib_wait_whole(zt):
        here = a_buf.at[CORES * zt + 1 - c]
        remote(here, here, sib_send.at[zt], sib_recv.at[zt, 0], i, sib).wait_recv()

    def sent(here, sem):
        remote(here, here, sem, sib_recv.at[0, 0], i, sib).wait_send()

    def own_to_sib():
        remote(xc_ref, there(z, c, META), meta_send.at[2, z], sib_recv.at[z, META], i, sib).start()
        remote(x_ref.at[:, 0], a_buf.at[j], sib_send.at[z], sib_recv.at[z, 0], i, sib).start()

    def row_part(n, k):
        h = STARTS[k] // HALF
        return halves[n][h].at[pl.ds(STARTS[k] - h * HALF, SIZES[k])]

    def to_rows(source, k):
        for n in range(2):
            remote(source, row_part(n, k), row_send.at[n], row_recv.at[n, k], (xn, yn)[n], j).start()

    def row_wait(n, k):
        here = row_part(n, k)
        remote(here, here, row_send.at[n], row_recv.at[n, k], xn, j).wait_recv()

    def dg_on(n):
        for k in RELAYED[n]:
            row_wait(n, k)
        for u in range(USED):
            relayed[n, u] = halves[n][n][slot_s[1, CORES * groups[1 + n] + n, u]]
        remote(relayed.at[n], used_part(dg_used, n), dg_send.at[n], dg_recv.at[n], (yn, xn)[n], j).start()

    def row_rest():
        for n in range(2):
            for k in range(PIECES):
                if k not in RELAYED[n]:
                    row_wait(n, k)
            remote(relayed.at[n], used_part(dg_used, n), dg_send.at[n], dg_recv.at[n], xn, j).wait_recv()

    def rows_sent():
        for n in range(2):
            sent(own_buf, row_send.at[n])
            sent(relayed.at[n], dg_send.at[n])

    def used_part(ref, h):
        return ref.at[pl.ds(h * USED, USED)]

    def table(r):
        return meta_v.at[pl.ds(TILES * r, TILES)]

    def table_out():
        for n in range(2):
            remote(table(i), table(i), tab_send.at[n], tab_recv.at[i], (xn, yn)[n], j).start()

    def table_wait(r):
        remote(table(r), table(r), tab_send.at[0], tab_recv.at[r], xn, j).wait_recv()

    def table_on():
        table_wait(xn)
        remote(table(xn), table(xn), tab_send.at[2], tab_recv.at[xn], yn, j).start()

    def table_rest():
        table_wait(yn)
        table_wait(dg)
        down = pltpu.make_async_copy(meta_v, meta_s, local.at[3])
        down.start()
        return down

    def find_slots():
        values = [
            jnp.concatenate([meta_v[TILES * r + t] for t in range(TILES)], axis=0) for r in range(STEPS)
        ]

        def largest(below):
            best = functools.reduce(
                jnp.maximum, [v if below is None else jnp.where(v < below, v, -1) for v in values]
            )
            best = jnp.max(best, axis=1, keepdims=True)
            return best if below is None else jnp.where(best < 0, below, best)

        high = largest(None)
        middle = largest(high)
        low = largest(middle)
        here = jnp.concatenate([meta_v[TILES * i + t] for t in range(TILES)], axis=0)
        slot_v[0, :, 0:ROWS] = jnp.where(here == high, 2, jnp.where(here == middle, 1, 0))
        lane_id = lax.broadcasted_iota(jnp.int32, (TILES, 128), 1)
        slot_v[1] = jnp.where(lane_id == 0, low, jnp.where(lane_id == 1, middle, high))
        slots_down = pltpu.make_async_copy(slot_v, slot_s, local.at[4])
        slots_down.start()
        slots_down.wait()

    def tables_sent():
        for n in range(3):
            sent(table(i), tab_send.at[n])

    def product(m, tile, pick, targets, which=range(STEPS)):
        lhs, rhs = [], []
        for g in which:
            for h in range(CORES):
                t = CORES * groups[g] + h
                at = h * HALF + meta_s[TILES * i + t, 0, m]
                block = pick(g, h, t, m)
                landing = meta_s[TILES * groups[g] + tile, 0, at]
                zero = jnp.zeros_like(block)
                rhs.append(jnp.concatenate([jnp.where(landing == targets[o, m], block, zero) for o in range(2)], axis=1))
                lhs.append(a_buf[t, m])
        return jnp.dot(
            jnp.concatenate(lhs, axis=1), jnp.concatenate(rhs, axis=0), preferred_element_type=jnp.float32
        )

    def from_whole(first):
        def pick(g, h, t, m):
            if g == STEPS - 1:
                return dg_used[h * USED + slot_s[0, t, m]]
            v = meta_s[TILES * i + t, 0, m]
            return first[h * HALF + v] if g == 0 else halves[g - 1][h][v]

        return pick

    def from_used(g, h, t, m):
        if g == 0:
            return own_buf[h * HALF + meta_s[TILES * i + t, 0, m]]
        return used[g - 1][h * USED + slot_s[0, t, m]]

    def store(ref, at, total):
        for o in range(2):
            ref[at, o] = total[:, o * 128 : (o + 1) * 128].astype(ref.dtype)

    def end_chip():
        z2, z3 = z_far, z + 3 * step

        def out():
            send_own(0, META)
            remote(oc_ref, oc_v, oc_send, oc_recv, i, toward[0]).start()
            for k in range(PIECES):
                send_own(0, k)

        pl.when(has_lower)(out)
        own_to_sib()

        def out_up():
            await_z()
            out()

        pl.when(has_upper)(out_up)
        await_row()
        for k in range(PIECES):
            to_rows(x_ref.at[part(k), 0], k)

        def arrived(zt, k):
            lane_wait(zt, k)
            to_sib(zt, k)

        arrived(z_mid, META)
        for k in KEPT_AT_END[:2]:
            arrived(z_mid, k)
        arrived(z2, META)
        arrived(z3, META)
        own_meta.wait()
        for zt in (z, z_mid, z2, z3):
            sib_wait(zt, META)
        table_out()
        for k in KEPT_AT_END[2:]:
            arrived(z_mid, k)
        table_on()
        down = table_rest()
        own.wait()
        own_again.wait()
        own_oc.wait()
        find_slots()
        dg_on(0)
        dg_on(1)
        for k in KEPT_AT_END:
            arrived(z2, k)
        row_rest()
        sib_wait_whole(z)
        down.wait()
        for k in KEPT_AT_END:
            for zt in (z_mid, z2):
                sib_wait(zt, k)
        for k in KEPT_AT_END:
            arrived(z3, k)
        for k in KEPT_AT_END:
            sib_wait(z3, k)

            def row(m, carry):
                store(o_ref, m, product(m, j, from_whole(own_buf), oc_s))
                return carry

            lax.fori_loop(STARTS[k], STARTS[k] + SIZES[k], row, 0, unroll=True)
        sent(there(z, c, META), meta_send.at[0, z])
        sent(oc_v, oc_send)
        sent(a_buf.at[j], lane_send.at[0, z])
        for zt in (z, z_mid, z2, z3):
            sent(there(zt, c, META), meta_send.at[2, zt])
        sent(a_buf.at[j], sib_send.at[z])
        for zt in (z_mid, z2, z3):
            sent(a_buf.at[j, pl.ds(LOW, HIGH - LOW)], sib_send.at[zt])
        rows_sent()
        tables_sent()
        for k in MOVED:
            here = o_ref.at[part(k)]
            remote(here, here, out_send, out_recv.at[k], i, sib).wait_recv()

    def inner_chip():
        def out_end():
            send_own(0, META)
            for k in KEPT_AT_END[:2]:
                send_own(0, k)

        def out_mid():
            for k in (META, 0, KEPT_AT_END[0]):
                send_own(1, k)

        pl.when(z == 1)(out_end)
        pl.when(z == 2)(out_mid)
        own_to_sib()
        await_z()
        pl.when(z == 1)(out_mid)
        pl.when(z == 2)(out_end)
        await_row()

        def from_end(k):
            lane_wait(z_end, k)
            if k != META:
                to_rows(a_buf.at[j_end, part(k)], k)
            send_on(1, z_end, k)
            to_sib(z_end, k)

        def from_mid(zt, k):
            lane_wait(zt, k)
            if k == META or k in KEPT_AT_END:
                send_on(0, zt, k)
            to_sib(zt, k)

        def used_out():
            for h in range(CORES):
                for n in range(USED):
                    own_used[h * USED + n] = own_buf[h * HALF + slot_s[1, CORES * i + h, n]]


            for n in range(2):
                for h in (n, 1 - n):
                    remote(
                        used_part(own_used, h), used_part(used[n], h), used_send.at[n], used_recv.at[n, h],
                        (xn, yn)[n], j,
                    ).start()

        def used_wait(n, h):
            dst = used_part(used[n], h)
            remote(dst, dst, used_fwd.at[0], used_recv.at[n, h], xn, j).wait_recv()

        def used_on(n):
            used_wait(n, n)
            remote(
                used_part(used[n], n), used_part(used[2], n), used_fwd.at[n], used_recv.at[2, n],
                (yn, xn)[n], j,
            ).start()

        def moved(k):
            for zt in (z_end, z_mid, z_far):
                sib_wait(zt, k)
            at = MOVED_ROWS.index(STARTS[k])

            def row(m, carry):
                store(result, m + at, product(m + STARTS[k], j_end, from_whole(end_buf), oc_out_s))
                return carry

            lax.fori_loop(0, SIZES[k], row, 0, unroll=True)
            remote(
                result.at[pl.ds(at, SIZES[k])], o_ref.at[part(k)], out_send, out_recv.at[k], i, toward[0]
            ).start()

        from_end(META)
        from_mid(z_mid, META)
        send_own(0, KEPT_AT_END[2])
        from_end(0)
        for k in KEPT_AT_END[1:]:
            send_own(1, k)
        from_mid(z_mid, 0)
        from_end(KEPT_AT_END[0])
        from_mid(z_mid, KEPT_AT_END[0])
        from_mid(z_far, META)
        for k in KEPT_AT_END[3:]:
            send_own(0, k)
        own_meta.wait()
        for zt in (z, z_end, z_mid, z_far):
            sib_wait(zt, META)
        table_out()
        from_mid(z_far, 0)
        from_end(KEPT_AT_END[1])
        from_mid(z_mid, KEPT_AT_END[1])
        table_on()
        from_end(KEPT_AT_END[2])
        from_mid(z_mid, KEPT_AT_END[2])
        for k in KEPT_AT_END[3:]:
            from_end(k)
            from_mid(z_mid, k)
        for k in MOVED[1:]:
            send_own(1, k)
            from_end(k)
        end_down = pltpu.make_async_copy(a_buf.at[j_end], end_buf, local.at[7])
        end_down.start()
        down = table_rest()
        own.wait()
        own_again.wait()
        find_slots()
        from_mid(z_far, KEPT_AT_END[0])
        dg_on(0)
        from_mid(z_far, KEPT_AT_END[1])
        dg_on(1)
        used_out()
        for k in KEPT_AT_END[2:]:
            from_mid(z_far, k)
        oc_wait = remote(oc_v, oc_v, oc_send, oc_recv, i, sib)
        oc_wait.wait_recv()
        oc_down = pltpu.make_async_copy(oc_v, oc_out_s, local.at[5])
        oc_down.start()
        down.wait()
        own_oc.wait()
        oc_down.wait()
        sib_wait_whole(z)
        for k in MOVED[1:]:
            from_mid(z_mid, k)
            from_mid(z_far, k)
        row_rest()
        end_down.wait()
        for k in MOVED:
            moved(k)
        used_on(0)
        used_on(1)
        for k in KEPT_AT_END:
            for zt in (z_end, z_mid, z_far):
                sib_wait(zt, k)
        for n in range(2):
            used_wait(n, 1 - n)

        def early(m, carry):
            acc[m] = product(m, j, from_used, oc_s, range(STEPS - 1))
            return carry

        lax.fori_loop(0, ROWS, early, 0, unroll=True)
        for n in range(2):
            used_wait(2, n)

        def row(m, carry):
            store(o_ref, m, acc[m] + product(m, j, from_used, oc_s, (STEPS - 1,)))
            return carry

        lax.fori_loop(0, ROWS, row, 0, unroll=True)
        for way, zts in enumerate(((z, z_mid, z_far), (z, z_end))):
            for zt in zts:
                sent(there(zt, c, META), meta_send.at[way, zt])
                whole = a_buf.at[0, pl.ds(LOW, HIGH - LOW)] if way == 0 else a_buf.at[0]
                sent(whole, lane_send.at[way, zt])
        for zt in (z, z_end, z_mid, z_far):
            sent(there(zt, c, META), meta_send.at[2, zt])
            sent(a_buf.at[0], sib_send.at[zt])
        rows_sent()
        tables_sent()
        for n in range(2):
            sent(own_used, used_send.at[n])
            sent(used_part(own_used, 0), used_fwd.at[n])
        sent(result, out_send)

    pl.when(inner)(inner_chip)
    pl.when(is_end)(end_chip)


def on_four_by_eight(xblocks, xcols, outcols):
    rows, _, size, _ = xblocks.shape
    kept = outcols.shape[1]
    dma = pltpu.SemaphoreType.DMA
    tile = (rows, size, size)
    return pl.pallas_call(
        kernel,
        out_shape=jax.ShapeDtypeStruct((rows, kept, size, size), jnp.bfloat16),
        in_specs=[pl.BlockSpec(memory_space=pltpu.HBM)] * 3,
        out_specs=pl.BlockSpec(memory_space=pltpu.VMEM),
        scratch_shapes=[
            pltpu.VMEM((TILES, *tile), jnp.bfloat16),
            *[pltpu.VMEM(tile, jnp.bfloat16)] * 2,
            *[pltpu.VMEM((HALF, size, size), jnp.bfloat16)] * 4,
            *[pltpu.VMEM((CORES * USED, size, size), jnp.bfloat16)] * 4,
            pltpu.VMEM((2, USED, size, size), jnp.bfloat16),
            pltpu.VMEM((CORES * USED, size, size), jnp.bfloat16),
            pltpu.VMEM((rows, size, kept * size), jnp.float32),
            pltpu.VMEM((len(MOVED_ROWS), kept, size, size), jnp.bfloat16),
            pltpu.VMEM((STEPS * TILES, 1, rows), jnp.int32),
            pltpu.VMEM((2, TILES, 128), jnp.int32),
            pltpu.VMEM((kept, rows), jnp.int32),
            pltpu.SMEM((STEPS * TILES, 1, rows), jnp.int32),
            pltpu.SMEM((2, TILES, 128), jnp.int32),
            pltpu.SMEM((kept, rows), jnp.int32),
            pltpu.SMEM((kept, rows), jnp.int32),
            dma((8,)),
            pltpu.SemaphoreType.REGULAR((3,)),
            dma((2, STEPS)),
            dma((STEPS, PIECES + 1)),
            dma((STEPS,)),
            dma((STEPS, PIECES + 1)),
            dma((3, STEPS)),
            dma((2,)),
            dma((2, PIECES)),
            dma((2,)),
            dma((2,)),
            dma((3,)),
            dma((STEPS,)),
            dma((2,)),
            dma((2,)),
            dma((3, 2)),
            dma,
            dma,
            dma,
            dma((PIECES,)),
        ],
        compiler_params=pltpu.CompilerParams(
            collective_id=0, has_side_effects=True, vmem_limit_bytes=32 * 1024 * 1024
        ),
    )(*(pltpu.with_memory_space_constraint(v, pltpu.HBM) for v in (xcols.T, outcols.T, xblocks)))


def solution(mesh):
    in_specs = (P("row", "col", None, None), P("row", "col"), P("row", "col"))
    out_specs = P("row", "col", None, None)
    fits = mesh.shape["row"] == STEPS and mesh.shape["col"] == CORES * STEPS
    body = on_four_by_eight if fits else on_any_mesh
    return jax.shard_map(body, mesh=mesh, in_specs=in_specs, out_specs=out_specs, check_vma=False)
```
